256 devices in a mesh: row: 32 (over x, z), col: 8 (over y, core).
Axes of the slice: x: 4, y: 4, z: 8, core: 2. Of those that a mesh axis runs over, the one named last changes fastest.
Arguments:
- covariance: float32 [16384, 16384], P('row', 'col'), as said below
- first_jacobian: bfloat16 [32, 16384], P(None, ('row', 'col')), may hold values from -0.046875 to 0.046875
- second_jacobian: bfloat16 [32, 16384], P(None, ('row', 'col')), may hold values from -0.046875 to 0.046875
- first_residuals: float32 [32], replicated, may hold values from -96 to 96
- second_residuals: float32 [32], replicated, may hold values from -48 to 48
Outputs:
- covariance_out: float32 [16384, 16384], P('row', 'col')
- increment: float32 [16384], P(('row', 'col'))
The draws below stay inside these ranges and needn't reach their ends.
Inputs may be any that keep to these rules, and one draw needn't show every extreme that they name: covariance is symmetric and positive definite, its diagonal between 3 and 6.
All inputs are finite; a program needn't handle non-finite values.
Results may differ from the reference program's by a relative error of at most 0.0003.
Values may be sent and summed in bfloat16 or wider, within the bound.
No kernel may reach another device: no remote copies, remote signals or barrier semaphores. Data moves between devices by JAX's collectives and lax.ppermute only.
A program may use at most 64 MiB of HBM per device.

```python
import jax
import jax.numpy as jnp
from jax import lax

PARAMETER_COUNT = 16384
MEASURE_COUNT = 32


def draw_covariance(key, part):
    first, second, third = jax.random.split(jax.random.fold_in(key, 7), 3)
    noise = jax.random.normal(first, (PARAMETER_COUNT, PARAMETER_COUNT), jnp.float32)
    sym = (noise + noise.T) * (0.35355339 / PARAMETER_COUNT ** 0.5)
    diagonal = jax.random.uniform(second, (PARAMETER_COUNT,), jnp.float32, 3.0, 6.0)
    half_count = PARAMETER_COUNT // 2
    coupling = jax.random.uniform(third, (half_count,), jnp.float32, 0.8, 1.2)
    coupling_full = jnp.concatenate([coupling, coupling])
    places = jnp.arange(PARAMETER_COUNT)
    partner = (places + half_count) % PARAMETER_COUNT
    sym = sym.at[places, partner].set(coupling_full)
    return sym.at[places, places].set(diagonal)


def block_scale(rng, extent, shards, low, largest):
    def one(position, shards_of):
        steps = jax.random.uniform(jax.random.fold_in(jax.random.fold_in(rng, 6), position), (shards_of,), jnp.float32, low / len(shards), largest / len(shards))
        return jnp.repeat(jnp.exp(steps), extent[position] // shards_of).reshape((-1,) + (1,) * (len(extent) - position - 1))

    factor_of = one(*shards[0])
    for cut in shards[1:]:
        factor_of = factor_of * one(*cut)
    return factor_of


def centred(own_key, dims, width, reach, shards=(), kind=jnp.bfloat16):
    drawn = width * jax.random.normal(own_key, dims, jnp.float32)
    if shards:
        drawn = drawn * block_scale(own_key, dims, shards, -0.22, 0.18)
    return jnp.clip(drawn, -reach, reach).astype(kind)


def setup_inputs(seed: int = 0) -> dict:
    splits = jax.random.split(jax.random.key(seed), 6)
    covariance = draw_covariance(jax.random.fold_in(splits[5], 71), 0)
    first_jacobian = centred(splits[1], (MEASURE_COUNT, PARAMETER_COUNT), PARAMETER_COUNT ** -0.5, 0.046875, ((1, 256),))
    second_jacobian = centred(splits[2], (MEASURE_COUNT, PARAMETER_COUNT), PARAMETER_COUNT ** -0.5, 0.046875, ((1, 256),))
    first_residuals = centred(splits[3], (MEASURE_COUNT,), 16.0, 96.0, (), jnp.float32)
    second_residuals = centred(splits[4], (MEASURE_COUNT,), 8.0, 48.0, (), jnp.float32)
    return dict(covariance=covariance, first_jacobian=first_jacobian, second_jacobian=second_jacobian, first_residuals=first_residuals, second_residuals=second_residuals)


lam_start = 0.98
forget_rate = 0.9987

def reference(covariance, first_jacobian, second_jacobian, first_residuals, second_residuals):
    current = covariance
    current_lambda = lam_start
    accum = jnp.zeros((PARAMETER_COUNT,), jnp.float32)
    previous = jnp.zeros((PARAMETER_COUNT,), jnp.float32)
    for jacobian, errors in ((first_jacobian, first_residuals), (second_jacobian, second_residuals)):
        widened_matrix = jacobian.astype(jnp.float32)
        covariance_product = jnp.dot(widened_matrix, current, precision=lax.Precision.HIGHEST)
        innovation_matrix = jnp.dot(covariance_product, widened_matrix.T, precision=lax.Precision.HIGHEST) + current_lambda * jnp.eye(MEASURE_COUNT, dtype=jnp.float32)
        predicted = jnp.dot(widened_matrix, previous, precision=lax.Precision.HIGHEST)
        factor = jnp.linalg.cholesky(innovation_matrix)
        solved = jax.scipy.linalg.cho_solve((factor, True), (errors - predicted)[:, None])[:, 0]
        delta = jnp.dot(covariance_product.T, solved, precision=lax.Precision.HIGHEST)
        gain = jax.scipy.linalg.cho_solve((factor, True), covariance_product)
        current = (current - jnp.dot(covariance_product.T, gain, precision=lax.Precision.HIGHEST)) / current_lambda
        accum = accum + delta
        previous = delta
        current_lambda = forget_rate * current_lambda + (1.0 - forget_rate)
    return (current, accum)
```

```python
import jax
import jax.numpy as jnp
from jax import lax
from jax.experimental import pallas as pl
from jax.experimental.pallas import tpu as pltpu
from jax.sharding import PartitionSpec as P

lam_start = 0.98
forget_rate = 0.9987
lam_next = forget_rate * lam_start + (1.0 - forget_rate)

f32 = jnp.float32
bf16 = jnp.bfloat16


def device(x, y, z, k):
    return (x * 8 + z) * 8 + y * 2 + k


def to_row_block(swap):
    pairs = []
    for x in range(4):
        for y in range(4):
            for z in range(8):
                for k in range(2):
                    i = ((z + 2 + 4 * k) % 8) // 2
                    target = device(y, (x + 2) % 4, 4 * k + i, (z + swap) % 2)
                    pairs.append((device(x, y, z, k), target))
    return pairs


def reversed_pairs(pairs):
    return [(b, a) for a, b in pairs]


def piece_at(tile, h, core):
    x = (tile % 4 + 2) % 4
    z = lax.rem(2 * (tile // 4) + h + 6 + 4 * core, 8)
    return x * 8 + z


def halves(value):
    hi = value.astype(bf16)
    return hi, (value - hi.astype(f32)).astype(bf16)


def thirds(value):
    hi = value.astype(bf16)
    rest = value - hi.astype(f32)
    mid = rest.astype(bf16)
    return hi, mid, (rest - mid.astype(f32)).astype(bf16)


def dot(a, b, dims):
    return lax.dot_general(a, b, (dims, ((), ())), preferred_element_type=f32)


def paired(even, odd):
    even, odd = even.astype(f32), odd.astype(f32)
    low = lax.broadcasted_iota(jnp.int32, even.shape, 1) < 64
    top = jnp.where(low, even, pltpu.roll(odd, 64, 1))
    bottom = jnp.where(low, pltpu.roll(even, 64, 1), odd)
    return jnp.concatenate([top, bottom], axis=0).astype(bf16)


VMEM = pl.BlockSpec(memory_space=pltpu.VMEM)


def product_kernel(jac_ref, cov_ref, out_ref):
    step = pl.program_id(0)
    core = lax.rem(lax.axis_index("col"), 2)
    jac = jnp.concatenate(
        [paired(jac_ref[2 * q], jac_ref[2 * q + 1]) for q in range(4)], axis=1
    )
    hi, mid, low = thirds(cov_ref[...])
    dims = ((1,), (0,))
    part = dot(jac, low, dims) + dot(jac, mid, dims) + dot(jac, hi, dims)
    for tile in range(4):
        for h in range(2):
            place = ((tile + 2) % 4) * 8 + lax.rem(2 * step + h + 6 + 4 * core, 8)
            out_ref[place] = part[32 * h : 32 * h + 32, 128 * tile : 128 * tile + 128]


def product(jac, cov):
    return pl.pallas_call(
        product_kernel,
        grid=(4,),
        in_specs=[
            pl.BlockSpec((8, 32, 128), lambda g: (0, 0, 0)),
            pl.BlockSpec((512, 512), lambda g: (0, g)),
        ],
        out_specs=pl.BlockSpec((32, 32, 128), lambda g: (0, 0, 0)),
        out_shape=jax.ShapeDtypeStruct((32, 32, 128), f32),
        name="product",
    )(jac, cov)


def reduce_kernel(parts_ref, same_ref, other_ref, row_ref, own_ref, gram_ref):
    total = jnp.sum(parts_ref[...], axis=0)
    own_ref[...] = total
    row_ref[...] = jnp.broadcast_to(total[None], row_ref.shape)
    second = lax.rem(lax.axis_index("row"), 2) == 1
    same, other = same_ref[...].astype(f32), other_ref[...].astype(f32)
    jac = paired(jnp.where(second, other, same), jnp.where(second, same, other))
    dims = ((1,), (1,))
    hi, mid, low = thirds(total)
    gram = dot(jac, low, dims) + dot(jac, mid, dims) + dot(jac, hi, dims)
    packed = jnp.concatenate([gram[16 * q : 16 * q + 16] for q in range(4)], axis=1)
    gram_ref[...] = jnp.broadcast_to(packed[None], gram_ref.shape)


def reduce(parts, same, other):
    return pl.pallas_call(
        reduce_kernel,
        in_specs=[VMEM] * 3,
        out_specs=[VMEM] * 3,
        out_shape=[
            jax.ShapeDtypeStruct((32, 32, 128), f32),
            jax.ShapeDtypeStruct((32, 128), f32),
            jax.ShapeDtypeStruct((8, 16, 128), f32),
        ],
        name="reduce",
    )(parts, same, other)


def spread_kernel(parts_ref, out_ref):
    total = jnp.sum(parts_ref[...], axis=0)
    out_ref[...] = jnp.broadcast_to(total[None], out_ref.shape)


def spread(parts):
    return pl.pallas_call(
        spread_kernel,
        in_specs=[VMEM],
        out_specs=VMEM,
        out_shape=jax.ShapeDtypeStruct((32, 16, 128), f32),
        name="spread",
    )(parts)


def factor_kernel(gram_ref, out_ref):
    first = gram_ref[0]
    second = gram_ref[1]
    for t in range(1, 16):
        first = first + gram_ref[2 * t]
        second = second + gram_ref[2 * t + 1]
    left = jnp.concatenate([first[:, 32 * q : 32 * q + 32] for q in range(4)], axis=0)
    right = jnp.concatenate([second[:, 32 * q : 32 * q + 32] for q in range(4)], axis=0)
    gram = jnp.concatenate([left, right, jnp.zeros((64, 64), f32)], axis=1)
    rows = lax.broadcasted_iota(jnp.int32, (64, 128), 0)
    lanes = lax.broadcasted_iota(jnp.int32, (64, 128), 1)
    shift = jnp.where(rows < 32, lam_start, lam_start * lam_next).astype(f32)
    work = gram + jnp.where(rows == lanes, shift, 0.0) + jnp.where(rows + 64 == lanes, 1.0, 0.0)
    diag = jnp.ones((64, 128), f32)
    for k in range(64):
        base = k // 8 * 8
        pivot_row = work[k : k + 1, :]
        pivot = pivot_row[:, k : k + 1]
        diag = jnp.where(rows == k, pivot, diag)
        if k == 63:
            break
        part = work[base:, :]
        column = part[:, k : k + 1] * (1.0 / pivot)
        column = jnp.where(rows[base:, :] > k, column, 0.0)
        part = part - column * pivot_row
        work = jnp.concatenate([work[:base, :], part], axis=0) if base else part
    out_ref[...] = work[:, 64:] * lax.rsqrt(diag)[:, :64]


def factor(gram):
    return pl.pallas_call(
        factor_kernel,
        in_specs=[VMEM],
        out_specs=VMEM,
        out_shape=jax.ShapeDtypeStruct((64, 64), f32),
        name="factor",
    )(gram)


def update_kernel(cov_ref, cols_ref, rows_ref, inv_ref, errors_ref, out_ref, inc_ref, left_ref):
    step = pl.program_id(0)
    core = lax.rem(lax.axis_index("col"), 2)
    highest = lax.Precision.HIGHEST

    def whitened(block):
        return jnp.dot(inv_ref[...], block, precision=highest, preferred_element_type=f32)

    @pl.when(step == 0)
    def _():
        rows = jnp.concatenate(
            [
                jnp.concatenate([rows_ref[2 * t], rows_ref[2 * t + 1]], axis=0)
                for t in range(4)
            ],
            axis=1,
        )
        rows = whitened(rows)
        hi, low = halves(rows)
        left_ref[...] = jnp.concatenate([hi, hi, low, low], axis=0)
        weights = jnp.sum(inv_ref[...] * errors_ref[...], axis=1, keepdims=True)
        inc_ref[...] = jnp.sum(rows * weights, axis=0, keepdims=True)

    pieces = []
    for tile in range(4):
        place = ((tile + 2) % 4) * 8
        turn = 2 * step + 6 + 4 * core
        pieces.append(
            jnp.concatenate(
                [cols_ref[place + lax.rem(turn + h, 8)] for h in range(2)], axis=0
            )
        )
    cols = whitened(jnp.concatenate(pieces, axis=1))
    hi, low = halves(cols)
    right = jnp.concatenate([hi, low, hi, low], axis=0)
    change = dot(left_ref[...], right, ((0,), (0,)))
    out_ref[...] = (cov_ref[...] - change) * (1.0 / (lam_start * lam_next))


def update(cov, cols, rows, inv, errors):
    return pl.pallas_call(
        update_kernel,
        grid=(4,),
        in_specs=[
            pl.BlockSpec((512, 512), lambda g: (0, g)),
            pl.BlockSpec((32, 32, 128), lambda g: (0, 0, 0)),
            pl.BlockSpec((8, 32, 128), lambda g: (0, 0, 0)),
            pl.BlockSpec((64, 64), lambda g: (0, 0)),
            pl.BlockSpec((1, 64), lambda g: (0, 0)),
        ],
        out_specs=[
            pl.BlockSpec((512, 512), lambda g: (0, g)),
            pl.BlockSpec((1, 512), lambda g: (0, 0)),
        ],
        out_shape=[
            jax.ShapeDtypeStruct((512, 2048), f32),
            jax.ShapeDtypeStruct((1, 512), f32),
        ],
        scratch_shapes=[pltpu.VMEM((256, 512), bf16)],
        name="update",
    )(cov, cols, rows, inv, errors)


def exchange(array, axis):
    return lax.all_to_all(array, axis, 0, 0, tiled=True)


def body(covariance, first_jacobian, second_jacobian, first_residuals, second_residuals):
    both = ("row", "col")
    jac = jnp.concatenate([first_jacobian, second_jacobian], axis=1)
    errors = jnp.concatenate([first_residuals, second_residuals])[None]
    jac_rows = exchange(jnp.broadcast_to(jac[None], (8, 32, 128)), "col")
    same = lax.ppermute(jac, both, reversed_pairs(to_row_block(0)))
    other = lax.ppermute(jac, both, reversed_pairs(to_row_block(1)))
    parts = exchange(product(jac_rows, covariance), "row")
    for_row, own, gram = reduce(parts, same, other)
    gram = exchange(gram, "col")
    cols = exchange(for_row, "row")
    natural = lax.ppermute(own, both, to_row_block(0))
    gram = exchange(spread(gram), "row")
    rows = exchange(jnp.broadcast_to(natural[None], (8, 32, 128)), "col")
    out, increment = update(covariance, cols, rows, factor(gram), errors)
    start = lax.axis_index("col") * 64
    return out, lax.dynamic_slice_in_dim(increment[0], start, 64, 0)


def solution(mesh):
    return jax.shard_map(
        body,
        mesh=mesh,
        in_specs=(P("row", "col"), P(None, ("row", "col")), P(None, ("row", "col")), P(), P()),
        out_specs=(P("row", "col"), P(("row", "col"))),
        check_vma=False,
    )
```

```python
import jax
import jax.numpy as jnp
from jax import lax
from jax.experimental import pallas as pl
from jax.experimental.pallas import tpu as pltpu
from jax.sharding import PartitionSpec as P

lam_start = 0.98
forget_rate = 0.9987
lam_next = forget_rate * lam_start + (1.0 - forget_rate)

f32 = jnp.float32
bf16 = jnp.bfloat16


def device(x, y, z, k):
    return (x * 8 + z) * 8 + y * 2 + k


def to_row_block(swap):
    pairs = []
    for x in range(4):
        for y in range(4):
            for z in range(8):
                for k in range(2):
                    i = ((z + 2 + 4 * k) % 8) // 2
                    target = device(y, (x + 2) % 4, 4 * k + i, (z + swap) % 2)
                    pairs.append((device(x, y, z, k), target))
    return pairs


def reversed_pairs(pairs):
    return [(b, a) for a, b in pairs]


def piece_at(tile, h, core):
    x = (tile % 4 + 2) % 4
    z = lax.rem(2 * (tile // 4) + h + 6 + 4 * core, 8)
    return x * 8 + z


def halves(value):
    hi = value.astype(bf16)
    return hi, (value - hi.astype(f32)).astype(bf16)


def thirds(value):
    hi = value.astype(bf16)
    rest = value - hi.astype(f32)
    mid = rest.astype(bf16)
    return hi, mid, (rest - mid.astype(f32)).astype(bf16)


def dot(a, b, dims):
    return lax.dot_general(a, b, (dims, ((), ())), preferred_element_type=f32)


def paired(even, odd):
    even, odd = even.astype(f32), odd.astype(f32)
    low = lax.broadcasted_iota(jnp.int32, even.shape, 1) < 64
    top = jnp.where(low, even, pltpu.roll(odd, 64, 1))
    bottom = jnp.where(low, pltpu.roll(even, 64, 1), odd)
    return jnp.concatenate([top, bottom], axis=0).astype(bf16)


VMEM = pl.BlockSpec(memory_space=pltpu.VMEM)
HBM = pl.BlockSpec(memory_space=pltpu.HBM)
GROUP = 256
GROUPS = 8


def group_of(ref, group):
    return ref.at[:, pl.ds(GROUP * group, GROUP)]


def start_loading(cov_ref, held_ref, sems):
    copies = [
        pltpu.make_async_copy(group_of(cov_ref, g), held_ref.at[g], sems.at[g])
        for g in range(GROUPS)
    ]
    for copy in copies:
        copy.start()
    return copies


def params(mib):
    return pltpu.CompilerParams(vmem_limit_bytes=int(mib * 1048576))


def product_kernel(jac_ref, cov_ref, out_ref, held_ref, sems):
    copies = start_loading(cov_ref, held_ref, sems)
    core = lax.rem(lax.axis_index("col"), 2)
    jac = jnp.concatenate(
        [paired(jac_ref[2 * q], jac_ref[2 * q + 1]) for q in range(4)], axis=1
    )
    dims = ((1,), (0,))
    for group in range(GROUPS):
        copies[group].wait()
        hi, mid, low = thirds(held_ref[group])
        part = dot(jac, low, dims) + dot(jac, mid, dims) + dot(jac, hi, dims)
        for half in range(2):
            tile = 2 * group + half
            for h in range(2):
                out_ref[piece_at(tile, h, core)] = part[
                    32 * h : 32 * h + 32, 128 * half : 128 * half + 128
                ]


def product(jac, cov):
    return pl.pallas_call(
        product_kernel,
        in_specs=[VMEM, HBM],
        out_specs=VMEM,
        out_shape=jax.ShapeDtypeStruct((32, 32, 128), f32),
        scratch_shapes=[
            pltpu.VMEM((GROUPS, 512, GROUP), f32),
            pltpu.SemaphoreType.DMA((GROUPS,)),
        ],
        compiler_params=params(60.25),
        name="product",
    )(jac, cov)


def reduce_kernel(parts_ref, same_ref, other_ref, row_ref, own_ref):
    total = jnp.sum(parts_ref[...], axis=0)
    own_ref[...] = total
    second = lax.rem(lax.axis_index("row"), 2) == 1
    same, other = same_ref[...].astype(f32), other_ref[...].astype(f32)
    jac = paired(jnp.where(second, other, same), jnp.where(second, same, other))
    dims = ((1,), (1,))
    hi, mid, low = thirds(total)
    gram = dot(jac, low, dims) + dot(jac, mid, dims) + dot(jac, hi, dims)
    packed = jnp.concatenate([gram[16 * q : 16 * q + 16] for q in range(4)], axis=1)
    row_ref[:, :32] = jnp.broadcast_to(total[None], (32, 32, 128))
    row_ref[:, 32:] = jnp.broadcast_to(packed[None], (32, 16, 128))


def reduce(parts, same, other):
    return pl.pallas_call(
        reduce_kernel,
        in_specs=[VMEM] * 3,
        out_specs=[VMEM] * 2,
        out_shape=[
            jax.ShapeDtypeStruct((32, 48, 128), f32),
            jax.ShapeDtypeStruct((32, 128), f32),
        ],
        compiler_params=params(8),
        name="reduce",
    )(parts, same, other)


def spread_kernel(parts_ref, natural_ref, out_ref):
    out_ref[:, :32] = jnp.broadcast_to(natural_ref[...][None], (8, 32, 128))
    for h in range(2):
        total = parts_ref[h, 32:]
        for t in range(1, 16):
            total = total + parts_ref[2 * t + h, 32:]
        out_ref[:, 32 + 16 * h : 48 + 16 * h] = jnp.broadcast_to(total[None], (8, 16, 128))


def spread(parts, natural):
    return pl.pallas_call(
        spread_kernel,
        in_specs=[VMEM] * 2,
        out_specs=VMEM,
        out_shape=jax.ShapeDtypeStruct((8, 64, 128), f32),
        compiler_params=params(4),
        name="spread",
    )(parts, natural)


PANEL = 4


def inverse_factor(total):
    first, second = total[:16], total[16:]
    left = jnp.concatenate([first[:, 32 * q : 32 * q + 32] for q in range(4)], axis=0)
    right = jnp.concatenate([second[:, 32 * q : 32 * q + 32] for q in range(4)], axis=0)
    gram = jnp.concatenate([left, right, jnp.zeros((64, 64), f32)], axis=1)
    rows = lax.broadcasted_iota(jnp.int32, (64, 128), 0)
    lanes = lax.broadcasted_iota(jnp.int32, (64, 128), 1)
    shift = jnp.where(rows < 32, lam_start, lam_start * lam_next).astype(f32)
    work = gram + jnp.where(rows == lanes, shift, 0.0) + jnp.where(rows + 64 == lanes, 1.0, 0.0)
    done = []
    for start in range(0, 64, PANEL):
        pivots = [work[j : j + 1, :] for j in range(PANEL)]
        rest = work[PANEL:, :]
        low = rest.shape[0]
        spots = range(start, start + PANEL)
        entry = {
            (i, j): jnp.broadcast_to(pivots[i][:, start + j : start + j + 1], (1, 128))
            for i in range(PANEL)
            for j in range(i + 1)
        }
        columns = [jnp.broadcast_to(rest[:, j : j + 1], (low, 128)) for j in spots] if low else []
        for j in range(PANEL):
            inverse = 1.0 / entry[j, j]
            factors = {i: entry[i, j] * inverse for i in range(j + 1, PANEL)}
            for i in range(j + 1, PANEL):
                pivots[i] = pivots[i] - factors[i] * pivots[j]
                for m in range(j + 1, i + 1):
                    entry[i, m] = entry[i, m] - factors[m] * entry[i, j]
                if low:
                    columns[i] = columns[i] - factors[i] * columns[j]
            done.append(pivots[j] * lax.rsqrt(entry[j, j]))
            if low:
                rest = rest - columns[j] * (pivots[j] * inverse)
        work = rest
    return jnp.concatenate(done, axis=0)[:, 64:]


def update_kernel(
    cov_ref, cols_ref, rows_ref, first_ref, second_ref, out_ref, inc_ref, held_ref, in_sems, out_sems
):
    loads = start_loading(cov_ref, held_ref, in_sems)
    col = lax.axis_index("col")
    core = lax.rem(col, 2)
    total = rows_ref[0, 32:]
    for c in range(1, 8):
        total = total + rows_ref[c, 32:]
    inverse = inverse_factor(total)
    hi, mid, low = thirds(inverse)
    inverse_parts = jnp.concatenate([hi, hi, hi, mid, mid, low], axis=1)

    def whitened(block):
        hi, mid, low = thirds(block)
        parts = jnp.concatenate([hi, mid, low, hi, mid, hi], axis=0)
        return dot(inverse_parts, parts, ((1,), (0,)))

    rows = whitened(
        jnp.concatenate(
            [
                jnp.concatenate([rows_ref[2 * t, :32], rows_ref[2 * t + 1, :32]], axis=0)
                for t in range(4)
            ],
            axis=1,
        )
    )
    hi, low = halves(rows.T)
    left = jnp.concatenate([hi, hi, low, low], axis=1)
    errors = jnp.concatenate([first_ref[...], second_ref[...]], axis=1)
    weights = jnp.sum(inverse * errors, axis=1, keepdims=True)
    inc = jnp.sum(rows * weights, axis=0, keepdims=True)
    own = jnp.zeros((1, 128), f32)
    for tile in range(4):
        own = own + jnp.where(col // 2 == tile, inc[:, 128 * tile : 128 * tile + 128], 0.0)
    inc_ref[...] = jnp.where(core == 1, own[:, 64:], own[:, :64])

    stores = []
    for group in range(GROUPS):
        pieces = [
            jnp.concatenate([cols_ref[piece_at(tile, h, core), :32] for h in range(2)], axis=0)
            for tile in (2 * group, 2 * group + 1)
        ]
        hi, low = halves(whitened(jnp.concatenate(pieces, axis=1)))
        change = dot(left, jnp.concatenate([hi, low, hi, low], axis=0), ((1,), (0,)))
        loads[group].wait()
        held_ref[group] = (held_ref[group] - change) * (1.0 / (lam_start * lam_next))
        store = pltpu.make_async_copy(
            held_ref.at[group], group_of(out_ref, group), out_sems.at[group]
        )
        store.start()
        stores.append(store)
    for store in stores:
        store.wait()


def update(cov, cols, rows, first, second):
    return pl.pallas_call(
        update_kernel,
        in_specs=[HBM] + [VMEM] * 4,
        out_specs=[HBM, VMEM],
        out_shape=[
            jax.ShapeDtypeStruct((512, 2048), f32),
            jax.ShapeDtypeStruct((1, 64), f32),
        ],
        scratch_shapes=[
            pltpu.VMEM((GROUPS, 512, GROUP), f32),
            pltpu.SemaphoreType.DMA((GROUPS,)),
            pltpu.SemaphoreType.DMA((GROUPS,)),
        ],
        compiler_params=params(60.25),
        name="update",
    )(cov, cols, rows, first, second)


def exchange(array, axis):
    return lax.all_to_all(array, axis, 0, 0, tiled=True)


def body(covariance, first_jacobian, second_jacobian, first_residuals, second_residuals):
    both = ("row", "col")
    jac = jnp.concatenate([first_jacobian, second_jacobian], axis=1)
    jac_rows = exchange(jnp.broadcast_to(jac[None], (8, 32, 128)), "col")
    same = lax.ppermute(jac, both, reversed_pairs(to_row_block(0)))
    other = lax.ppermute(jac, both, reversed_pairs(to_row_block(1)))
    parts = product(jac_rows, covariance)
    parts = exchange(parts, "row")
    for_row, own = reduce(parts, same, other)
    cols = exchange(for_row, "row")
    natural = lax.ppermute(own, both, to_row_block(0))
    rows = exchange(spread(cols, natural), "col")
    out, increment = update(covariance, cols, rows, first_residuals[None], second_residuals[None])
    return out, increment[0]


def solution(mesh):
    return jax.shard_map(
        body,
        mesh=mesh,
        in_specs=(P("row", "col"), P(None, ("row", "col")), P(None, ("row", "col")), P(), P()),
        out_specs=(P("row", "col"), P(("row", "col"))),
        check_vma=False,
    )
```

```python
import jax
import jax.numpy as jnp
from jax import lax
from jax.experimental import pallas as pl
from jax.experimental.pallas import tpu as pltpu
from jax.sharding import PartitionSpec as P


lam_start = 0.98
forget_rate = 0.9987
lam_next = forget_rate * lam_start + (1.0 - forget_rate)

f32 = jnp.float32
bf16 = jnp.bfloat16


def device(x, y, z, k):
    return (x * 8 + z) * 8 + y * 2 + k


def to_row_block(swap):
    pairs = []
    for x in range(4):
        for y in range(4):
            for z in range(8):
                for k in range(2):
                    i = ((z + 2 + 4 * k) % 8) // 2
                    target = device(y, (x + 2) % 4, 4 * k + i, (z + swap) % 2)
                    pairs.append((device(x, y, z, k), target))
    return pairs


def reversed_pairs(pairs):
    return [(b, a) for a, b in pairs]


def piece_at(tile, h, core):
    x = (tile % 4 + 2) % 4
    z = lax.rem(2 * (tile // 4) + h + 6 + 4 * core, 8)
    return x * 8 + z


def halves(value):
    hi = value.astype(bf16)
    return hi, (value - hi.astype(f32)).astype(bf16)


def thirds(value):
    hi = value.astype(bf16)
    rest = value - hi.astype(f32)
    mid = rest.astype(bf16)
    return hi, mid, (rest - mid.astype(f32)).astype(bf16)


def dot(a, b, dims):
    return lax.dot_general(a, b, (dims, ((), ())), preferred_element_type=f32)


def paired(even, odd):
    even, odd = even.astype(f32), odd.astype(f32)
    low = lax.broadcasted_iota(jnp.int32, even.shape, 1) < 64
    top = jnp.where(low, even, pltpu.roll(odd, 64, 1))
    bottom = jnp.where(low, pltpu.roll(even, 64, 1), odd)
    return jnp.concatenate([top, bottom], axis=0).astype(bf16)


VMEM = pl.BlockSpec(memory_space=pltpu.VMEM)
HBM = pl.BlockSpec(memory_space=pltpu.HBM)
GROUP = 512
GROUPS = 4


def group_of(ref, group):
    return ref.at[:, pl.ds(GROUP * group, GROUP)]


def start_loading(cov_ref, held_ref, sems):
    copies = [
        pltpu.make_async_copy(group_of(cov_ref, g), held_ref.at[g], sems.at[g])
        for g in range(GROUPS)
    ]
    for copy in copies:
        copy.start()
    return copies


def params(mib):
    return pltpu.CompilerParams(vmem_limit_bytes=int(mib * 1048576))


def product_kernel(jac_ref, cov_ref, out_ref, held_ref, sems):
    copies = start_loading(cov_ref, held_ref, sems)
    core = lax.rem(lax.axis_index("col"), 2)
    jac = jnp.concatenate(
        [paired(jac_ref[2 * q], jac_ref[2 * q + 1]) for q in range(4)], axis=1
    )
    dims = ((1,), (0,))
    for group in range(GROUPS):
        copies[group].wait()
        hi, low = halves(held_ref[group])
        part = dot(jac, low, dims) + dot(jac, hi, dims)
        for step in range(GROUP // 128):
            for h in range(2):
                place = piece_at(GROUP // 128 * group + step, h, core)
                out_ref[place] = part[32 * h : 32 * h + 32, 128 * step : 128 * step + 128]


def product(jac, cov):
    return pl.pallas_call(
        product_kernel,
        in_specs=[VMEM, HBM],
        out_specs=VMEM,
        out_shape=jax.ShapeDtypeStruct((32, 32, 128), f32),
        scratch_shapes=[
            pltpu.VMEM((GROUPS, 512, GROUP), f32),
            pltpu.SemaphoreType.DMA((GROUPS,)),
        ],
        compiler_params=params(60.25),
        name="product",
    )(jac, cov)


def reduce_kernel(parts_ref, same_ref, other_ref, row_ref, own_ref):
    total = jnp.sum(parts_ref[...], axis=0)
    own_ref[...] = total
    second = lax.rem(lax.axis_index("row"), 2) == 1
    same, other = same_ref[...].astype(f32), other_ref[...].astype(f32)
    jac = paired(jnp.where(second, other, same), jnp.where(second, same, other))
    dims = ((1,), (1,))
    hi, mid, low = thirds(total)
    gram = dot(jac, low, dims) + dot(jac, mid, dims) + dot(jac, hi, dims)
    packed = jnp.concatenate([gram[16 * q : 16 * q + 16] for q in range(4)], axis=1)
    row_ref[:, :32] = jnp.broadcast_to(total[None], (32, 32, 128))
    row_ref[:, 32:] = jnp.broadcast_to(packed[None], (32, 16, 128))


def reduce(parts, same, other):
    return pl.pallas_call(
        reduce_kernel,
        in_specs=[VMEM] * 3,
        out_specs=[VMEM] * 2,
        out_shape=[
            jax.ShapeDtypeStruct((32, 48, 128), f32),
            jax.ShapeDtypeStruct((32, 128), f32),
        ],
        compiler_params=params(8),
        name="reduce",
    )(parts, same, other)


def spread_kernel(parts_ref, natural_ref, out_ref):
    out_ref[:, :32] = jnp.broadcast_to(natural_ref[...][None], (8, 32, 128))
    for h in range(2):
        total = parts_ref[h, 32:]
        for t in range(1, 16):
            total = total + parts_ref[2 * t + h, 32:]
        out_ref[:, 32 + 16 * h : 48 + 16 * h] = jnp.broadcast_to(total[None], (8, 16, 128))


def spread(parts, natural):
    return pl.pallas_call(
        spread_kernel,
        in_specs=[VMEM] * 2,
        out_specs=VMEM,
        out_shape=jax.ShapeDtypeStruct((8, 64, 128), f32),
        compiler_params=params(4),
        name="spread",
    )(parts, natural)


PANEL = 8


def inverse_factor(total):
    first, second = total[:16], total[16:]
    left = jnp.concatenate([first[:, 32 * q : 32 * q + 32] for q in range(4)], axis=0)
    right = jnp.concatenate([second[:, 32 * q : 32 * q + 32] for q in range(4)], axis=0)
    gram = jnp.concatenate([left, right, jnp.zeros((64, 64), f32)], axis=1)
    rows = lax.broadcasted_iota(jnp.int32, (64, 128), 0)
    lanes = lax.broadcasted_iota(jnp.int32, (64, 128), 1)
    shift = jnp.where(rows < 32, lam_start, lam_start * lam_next).astype(f32)
    work = gram + jnp.where(rows == lanes, shift, 0.0) + jnp.where(rows + 64 == lanes, 1.0, 0.0)
    done = []
    for start in range(0, 64, PANEL):
        pivots = [work[j : j + 1, :] for j in range(PANEL)]
        rest = work[PANEL:, :]
        low = rest.shape[0]
        spots = range(start, start + PANEL)
        entry = {
            (i, j): jnp.broadcast_to(pivots[i][:, start + j : start + j + 1], (1, 128))
            for i in range(PANEL)
            for j in range(i + 1)
        }
        columns = [jnp.broadcast_to(rest[:, j : j + 1], (low, 128)) for j in spots] if low else []
        for j in range(PANEL):
            inverse = 1.0 / entry[j, j]
            factors = {i: entry[i, j] * inverse for i in range(j + 1, PANEL)}
            for i in range(j + 1, PANEL):
                pivots[i] = pivots[i] - factors[i] * pivots[j]
                for m in range(j + 1, i + 1):
                    entry[i, m] = entry[i, m] - factors[m] * entry[i, j]
                if low:
                    columns[i] = columns[i] - factors[i] * columns[j]
            done.append(pivots[j] * lax.rsqrt(entry[j, j]))
            if low:
                rest = rest - columns[j] * (pivots[j] * inverse)
        work = rest
    return jnp.concatenate(done, axis=0)[:, 64:]


def update_kernel(
    cov_ref, cols_ref, rows_ref, first_ref, second_ref, out_ref, inc_ref, held_ref, in_sems, out_sems
):
    loads = start_loading(cov_ref, held_ref, in_sems)
    col = lax.axis_index("col")
    core = lax.rem(col, 2)
    total = rows_ref[0, 32:]
    for c in range(1, 8):
        total = total + rows_ref[c, 32:]
    inverse = inverse_factor(total)
    hi, mid, low = thirds(inverse)
    inverse_parts = jnp.concatenate([hi, hi, hi, mid, mid, low], axis=1)

    def whitened(block):
        hi, mid, low = thirds(block)
        parts = jnp.concatenate([hi, mid, low, hi, mid, hi], axis=0)
        return dot(inverse_parts, parts, ((1,), (0,)))

    rows = whitened(
        jnp.concatenate(
            [
                jnp.concatenate([rows_ref[2 * t, :32], rows_ref[2 * t + 1, :32]], axis=0)
                for t in range(4)
            ],
            axis=1,
        )
    )
    hi, low = halves(rows.T)
    left = jnp.concatenate([hi, hi, low, low], axis=1)
    errors = jnp.concatenate([first_ref[...], second_ref[...]], axis=1)
    weights = jnp.sum(inverse * errors, axis=1, keepdims=True)
    inc = jnp.sum(rows * weights, axis=0, keepdims=True)
    own = jnp.zeros((1, 128), f32)
    for tile in range(4):
        own = own + jnp.where(col // 2 == tile, inc[:, 128 * tile : 128 * tile + 128], 0.0)
    inc_ref[...] = jnp.where(core == 1, own[:, 64:], own[:, :64])

    cols = whitened(
        jnp.concatenate(
            [
                jnp.concatenate([cols_ref[piece_at(tile, h, core), :32] for h in range(2)], axis=0)
                for tile in range(16)
            ],
            axis=1,
        )
    )
    hi, low = halves(cols)
    right = jnp.concatenate([hi, low, hi, low], axis=0)
    for load in loads:
        load.wait()
    stores = []
    for group in range(GROUPS):
        change = dot(left, right[:, GROUP * group : GROUP * group + GROUP], ((1,), (0,)))
        held_ref[group] = (held_ref[group] - change) * (1.0 / (lam_start * lam_next))
        store = pltpu.make_async_copy(
            held_ref.at[group], group_of(out_ref, group), out_sems.at[group]
        )
        store.start()
        stores.append(store)
    for store in stores:
        store.wait()


def update(cov, cols, rows, first, second):
    return pl.pallas_call(
        update_kernel,
        in_specs=[HBM] + [VMEM] * 4,
        out_specs=[HBM, VMEM],
        out_shape=[
            jax.ShapeDtypeStruct((512, 2048), f32),
            jax.ShapeDtypeStruct((1, 64), f32),
        ],
        scratch_shapes=[
            pltpu.VMEM((GROUPS, 512, GROUP), f32),
            pltpu.SemaphoreType.DMA((GROUPS,)),
            pltpu.SemaphoreType.DMA((GROUPS,)),
        ],
        compiler_params=params(60.25),
        name="update",
    )(cov, cols, rows, first, second)


def exchange(array, axis):
    return lax.all_to_all(array, axis, 0, 0, tiled=True)


def body(covariance, first_jacobian, second_jacobian, first_residuals, second_residuals):
    both = ("row", "col")
    jac = jnp.concatenate([first_jacobian, second_jacobian], axis=1)
    jac_rows = exchange(jnp.broadcast_to(jac[None], (8, 32, 128)), "col")
    same = lax.ppermute(jac, both, reversed_pairs(to_row_block(0)))
    other = lax.ppermute(jac, both, reversed_pairs(to_row_block(1)))
    parts = product(jac_rows, covariance)
    parts = exchange(parts, "row")
    for_row, own = reduce(parts, same, other)
    cols = exchange(for_row, "row")
    natural = lax.ppermute(own, both, to_row_block(0))
    rows = exchange(spread(cols, natural), "col")
    out, increment = update(covariance, cols, rows, first_residuals[None], second_residuals[None])
    return out, increment[0]


def solution(mesh):
    return jax.shard_map(
        body,
        mesh=mesh,
        in_specs=(P("row", "col"), P(None, ("row", "col")), P(None, ("row", "col")), P(), P()),
        out_specs=(P("row", "col"), P(("row", "col"))),
        check_vma=False,
    )
```

```python
import jax
import jax.numpy as jnp
from jax import lax
from jax.experimental import pallas as pl
from jax.experimental.pallas import tpu as pltpu
from jax.sharding import PartitionSpec as P


lam_start = 0.98
forget_rate = 0.9987
lam_next = forget_rate * lam_start + (1.0 - forget_rate)

f32 = jnp.float32
bf16 = jnp.bfloat16


def device(x, y, z, k):
    return (x * 8 + z) * 8 + y * 2 + k


def to_row_block():
    pairs = []
    for x in range(4):
        for y in range(4):
            for z in range(8):
                for k in range(2):
                    i = ((z + 2 + 4 * k) % 8) // 2
                    target = device(y, (x + 2) % 4, 4 * k + i, z % 2)
                    pairs.append((device(x, y, z, k), target))
    return pairs


def reversed_pairs(pairs):
    return [(b, a) for a, b in pairs]


def piece_at(tile, h, core):
    x = (tile % 4 + 2) % 4
    z = lax.rem(2 * (tile // 4) + h + 6 + 4 * core, 8)
    return x * 8 + z


def halves(value):
    hi = value.astype(bf16)
    return hi, (value - hi.astype(f32)).astype(bf16)


def thirds(value):
    hi = value.astype(bf16)
    rest = value - hi.astype(f32)
    mid = rest.astype(bf16)
    return hi, mid, (rest - mid.astype(f32)).astype(bf16)


def dot(a, b, dims):
    return lax.dot_general(a, b, (dims, ((), ())), preferred_element_type=f32)


def paired(even, odd):
    even, odd = even.astype(f32), odd.astype(f32)
    low = lax.broadcasted_iota(jnp.int32, even.shape, 1) < 64
    top = jnp.where(low, even, pltpu.roll(odd, 64, 1))
    bottom = jnp.where(low, pltpu.roll(even, 64, 1), odd)
    return jnp.concatenate([top, bottom], axis=0).astype(bf16)


VMEM = pl.BlockSpec(memory_space=pltpu.VMEM)
HBM = pl.BlockSpec(memory_space=pltpu.HBM)
GROUP = 512
GROUPS = 4


def group_of(ref, group):
    return ref.at[:, pl.ds(GROUP * group, GROUP)]


def start_loading(cov_ref, held_ref, sems):
    copies = [
        pltpu.make_async_copy(group_of(cov_ref, g), held_ref.at[g], sems.at[g])
        for g in range(GROUPS)
    ]
    for copy in copies:
        copy.start()
    return copies


def params(mib):
    return pltpu.CompilerParams(vmem_limit_bytes=int(mib * 1048576))


EARLY = 3


def load_kernel(cov_ref, out_ref, sems):
    copies = [
        pltpu.make_async_copy(group_of(cov_ref, g), out_ref.at[g], sems.at[g])
        for g in range(EARLY)
    ]
    for copy in copies:
        copy.start()
    for copy in copies:
        copy.wait()


def load(cov):
    return pl.pallas_call(
        load_kernel,
        in_specs=[HBM],
        out_specs=VMEM,
        out_shape=jax.ShapeDtypeStruct((EARLY, 512, GROUP), f32),
        scratch_shapes=[pltpu.SemaphoreType.DMA((EARLY,))],
        compiler_params=params(16),
        name="load",
    )(cov)


def product_kernel(jac_ref, early_ref, cov_ref, out_ref, own_ref, late_ref, sems):
    copies = [
        pltpu.make_async_copy(group_of(cov_ref, g), late_ref.at[g - EARLY], sems.at[g - EARLY])
        for g in range(EARLY, GROUPS)
    ]
    for copy in copies:
        copy.start()
    col = lax.axis_index("col")
    core = lax.rem(col, 2)
    blocks = [paired(jac_ref[2 * q], jac_ref[2 * q + 1]) for q in range(4)]
    own = blocks[0]
    for q in range(1, 4):
        own = jnp.where(col // 2 == q, blocks[q], own)
    own_ref[...] = own
    jac = jnp.concatenate(blocks, axis=1)
    dims = ((1,), (0,))
    for group in range(GROUPS):
        if group >= EARLY:
            copies[group - EARLY].wait()
        hi, low = halves(early_ref[group] if group < EARLY else late_ref[group - EARLY])
        part = dot(jac, low, dims) + dot(jac, hi, dims)
        for step in range(GROUP // 128):
            for h in range(2):
                place = piece_at(GROUP // 128 * group + step, h, core)
                out_ref[place] = part[32 * h : 32 * h + 32, 128 * step : 128 * step + 128]


def product(jac, early, cov):
    return pl.pallas_call(
        product_kernel,
        in_specs=[VMEM, VMEM, HBM],
        out_specs=[VMEM] * 2,
        out_shape=[
            jax.ShapeDtypeStruct((32, 32, 128), f32),
            jax.ShapeDtypeStruct((64, 128), bf16),
        ],
        scratch_shapes=[
            pltpu.VMEM((GROUPS - EARLY, 512, GROUP), f32),
            pltpu.SemaphoreType.DMA((GROUPS - EARLY,)),
        ],
        compiler_params=params(16),
        name="product",
    )(jac, early, cov)


def reduce_kernel(parts_ref, jac_ref, own_ref, kept_ref, sent_ref):
    total = jnp.sum(parts_ref[...], axis=0)
    own_ref[...] = total
    dims = ((1,), (1,))
    hi, mid, low = thirds(total)
    jac = jac_ref[...]
    gram = dot(jac, low, dims) + dot(jac, mid, dims) + dot(jac, hi, dims)
    packed = jnp.concatenate([gram[16 * q : 16 * q + 16] for q in range(4)], axis=1)
    first = lax.rem(lax.axis_index("col"), 2) == 0
    kept_ref[...] = jnp.where(first, packed[:8], packed[8:])
    sent_ref[...] = jnp.where(first, packed[8:], packed[:8])


def reduce(parts, jac):
    return pl.pallas_call(
        reduce_kernel,
        in_specs=[VMEM] * 2,
        out_specs=[VMEM] * 3,
        out_shape=[
            jax.ShapeDtypeStruct((32, 128), f32),
            jax.ShapeDtypeStruct((8, 128), f32),
            jax.ShapeDtypeStruct((8, 128), f32),
        ],
        compiler_params=params(8),
        name="reduce",
    )(parts, jac)


def fill_kernel(own_ref, kept_ref, got_ref, out_ref):
    out_ref[:, :32] = jnp.broadcast_to(own_ref[...][None], (32, 32, 128))
    gram = kept_ref[...] + got_ref[...]
    out_ref[:, 32:] = jnp.broadcast_to(gram[None], (32, 8, 128))


def fill(own, kept, got):
    return pl.pallas_call(
        fill_kernel,
        in_specs=[VMEM] * 3,
        out_specs=VMEM,
        out_shape=jax.ShapeDtypeStruct((32, 40, 128), f32),
        compiler_params=params(8),
        name="fill",
    )(own, kept, got)


def spread_kernel(parts_ref, natural_ref, out_ref):
    out_ref[:, :32] = jnp.broadcast_to(natural_ref[...][None], (8, 32, 128))
    for h in range(2):
        total = parts_ref[h, 32:]
        for t in range(1, 16):
            total = total + parts_ref[2 * t + h, 32:]
        out_ref[:, 32 + 8 * h : 40 + 8 * h] = jnp.broadcast_to(total[None], (8, 8, 128))


def spread(parts, natural):
    return pl.pallas_call(
        spread_kernel,
        in_specs=[VMEM] * 2,
        out_specs=VMEM,
        out_shape=jax.ShapeDtypeStruct((8, 48, 128), f32),
        compiler_params=params(4),
        name="spread",
    )(parts, natural)


PANEL = 8


def inverse_factor(first, second):
    left = jnp.concatenate([first[:, 32 * q : 32 * q + 32] for q in range(4)], axis=0)
    right = jnp.concatenate([second[:, 32 * q : 32 * q + 32] for q in range(4)], axis=0)
    gram = jnp.concatenate([left, right, jnp.zeros((64, 64), f32)], axis=1)
    rows = lax.broadcasted_iota(jnp.int32, (64, 128), 0)
    lanes = lax.broadcasted_iota(jnp.int32, (64, 128), 1)
    shift = jnp.where(rows < 32, lam_start, lam_start * lam_next).astype(f32)
    work = gram + jnp.where(rows == lanes, shift, 0.0) + jnp.where(rows + 64 == lanes, 1.0, 0.0)
    done = []
    for start in range(0, 64, PANEL):
        pivots = [work[j : j + 1, :] for j in range(PANEL)]
        rest = work[PANEL:, :]
        low = rest.shape[0]
        spots = range(start, start + PANEL)
        entry = {
            (i, j): jnp.broadcast_to(pivots[i][:, start + j : start + j + 1], (1, 128))
            for i in range(PANEL)
            for j in range(i + 1)
        }
        columns = [jnp.broadcast_to(rest[:, j : j + 1], (low, 128)) for j in spots] if low else []
        for j in range(PANEL):
            inverse = 1.0 / entry[j, j]
            factors = {i: entry[i, j] * inverse for i in range(j + 1, PANEL)}
            for i in range(j + 1, PANEL):
                pivots[i] = pivots[i] - factors[i] * pivots[j]
                for m in range(j + 1, i + 1):
                    entry[i, m] = entry[i, m] - factors[m] * entry[i, j]
                if low:
                    columns[i] = columns[i] - factors[i] * columns[j]
            done.append(pivots[j] * lax.rsqrt(entry[j, j]))
            if low:
                rest = rest - columns[j] * (pivots[j] * inverse)
        work = rest
    return jnp.concatenate(done, axis=0)[:, 64:]


def update_kernel(
    cov_ref, cols_ref, rows_ref, first_ref, second_ref, out_ref, inc_ref, held_ref, in_sems, out_sems
):
    loads = start_loading(cov_ref, held_ref, in_sems)
    col = lax.axis_index("col")
    core = lax.rem(col, 2)
    first, second = [
        jnp.concatenate(
            [
                sum(rows_ref[2 * y + k, 32 + 8 * h : 40 + 8 * h] for y in range(1, 4))
                + rows_ref[k, 32 + 8 * h : 40 + 8 * h]
                for k in range(2)
            ],
            axis=0,
        )
        for h in range(2)
    ]
    inverse = inverse_factor(first, second)
    hi, mid, low = thirds(inverse)
    inverse_parts = jnp.concatenate([hi, hi, hi, mid, mid, low], axis=1)

    def whitened(block):
        hi, mid, low = thirds(block)
        parts = jnp.concatenate([hi, mid, low, hi, mid, hi], axis=0)
        return dot(inverse_parts, parts, ((1,), (0,)))

    rows = whitened(
        jnp.concatenate(
            [
                jnp.concatenate([rows_ref[2 * t, :32], rows_ref[2 * t + 1, :32]], axis=0)
                for t in range(4)
            ],
            axis=1,
        )
    )
    hi, low = halves(rows.T)
    left = jnp.concatenate([hi, hi, low, low], axis=1)
    errors = jnp.concatenate([first_ref[...], second_ref[...]], axis=1)
    weights = jnp.sum(inverse * errors, axis=1, keepdims=True)
    inc = jnp.sum(rows * weights, axis=0, keepdims=True)
    own = jnp.zeros((1, 128), f32)
    for tile in range(4):
        own = own + jnp.where(col // 2 == tile, inc[:, 128 * tile : 128 * tile + 128], 0.0)
    inc_ref[...] = jnp.where(core == 1, own[:, 64:], own[:, :64])

    cols = whitened(
        jnp.concatenate(
            [
                jnp.concatenate([cols_ref[piece_at(tile, h, core), :32] for h in range(2)], axis=0)
                for tile in range(16)
            ],
            axis=1,
        )
    )
    hi, low = halves(cols)
    right = jnp.concatenate([hi, low, hi, low], axis=0)
    for load in loads:
        load.wait()
    stores = []
    for group in range(GROUPS):
        change = dot(left, right[:, GROUP * group : GROUP * group + GROUP], ((1,), (0,)))
        held_ref[group] = (held_ref[group] - change) * (1.0 / (lam_start * lam_next))
        store = pltpu.make_async_copy(
            held_ref.at[group], group_of(out_ref, group), out_sems.at[group]
        )
        store.start()
        stores.append(store)
    for store in stores:
        store.wait()


def update(cov, cols, rows, first, second):
    return pl.pallas_call(
        update_kernel,
        in_specs=[HBM] + [VMEM] * 4,
        out_specs=[HBM, VMEM],
        out_shape=[
            jax.ShapeDtypeStruct((512, 2048), f32),
            jax.ShapeDtypeStruct((1, 64), f32),
        ],
        scratch_shapes=[
            pltpu.VMEM((GROUPS, 512, GROUP), f32),
            pltpu.SemaphoreType.DMA((GROUPS,)),
            pltpu.SemaphoreType.DMA((GROUPS,)),
        ],
        compiler_params=params(16),
        name="update",
    )(cov, cols, rows, first, second)


def exchange(array, axis):
    return lax.all_to_all(array, axis, 0, 0, tiled=True)


def body(covariance, first_jacobian, second_jacobian, first_residuals, second_residuals):
    both = ("row", "col")
    jac = jnp.concatenate([first_jacobian, second_jacobian], axis=1)
    jac_rows = exchange(jnp.broadcast_to(jac[None], (8, 32, 128)), "col")
    covariance = pltpu.with_memory_space_constraint(covariance, pltpu.HBM)
    held = load(covariance)
    parts, jac_own = product(jac_rows, held, covariance)
    parts = exchange(parts, "row")
    jac_piece = lax.ppermute(jac_own, both, reversed_pairs(to_row_block()))
    own, kept, sent = reduce(parts, jac_piece)
    got = lax.ppermute(sent, "col", [(c, c ^ 1) for c in range(8)])
    cols = exchange(fill(own, kept, got), "row")
    natural = lax.ppermute(own, both, to_row_block())
    rows = exchange(spread(cols, natural), "col")
    out, increment = update(covariance, cols, rows, first_residuals[None], second_residuals[None])
    return out, increment[0]


def solution(mesh):
    return jax.shard_map(
        body,
        mesh=mesh,
        in_specs=(P("row", "col"), P(None, ("row", "col")), P(None, ("row", "col")), P(), P()),
        out_specs=(P("row", "col"), P(("row", "col"))),
        check_vma=False,
    )
```

```python
import jax
import jax.numpy as jnp
from jax import lax
from jax.experimental import pallas as pl
from jax.experimental.pallas import tpu as pltpu
from jax.sharding import PartitionSpec as P


lam_start = 0.98
forget_rate = 0.9987
lam_next = forget_rate * lam_start + (1.0 - forget_rate)

f32 = jnp.float32
bf16 = jnp.bfloat16


def device(x, y, z, k):
    return (x * 8 + z) * 8 + y * 2 + k


def to_row_block(swap):
    pairs = []
    for x in range(4):
        for y in range(4):
            for z in range(8):
                for k in range(2):
                    i = ((z + 2 + 4 * k) % 8) // 2
                    target = device(y, (x + 2) % 4, 4 * k + i, (z + swap) % 2)
                    pairs.append((device(x, y, z, k), target))
    return pairs


def reversed_pairs(pairs):
    return [(b, a) for a, b in pairs]


def piece_at(tile, h, core):
    x = (tile % 4 + 2) % 4
    z = lax.rem(2 * (tile // 4) + h + 6 + 4 * core, 8)
    return x * 8 + z


def halves(value):
    hi = value.astype(bf16)
    return hi, (value - hi.astype(f32)).astype(bf16)


def thirds(value):
    hi = value.astype(bf16)
    rest = value - hi.astype(f32)
    mid = rest.astype(bf16)
    return hi, mid, (rest - mid.astype(f32)).astype(bf16)


def dot(a, b, dims):
    return lax.dot_general(a, b, (dims, ((), ())), preferred_element_type=f32)


def paired(even, odd):
    even, odd = even.astype(f32), odd.astype(f32)
    low = lax.broadcasted_iota(jnp.int32, even.shape, 1) < 64
    top = jnp.where(low, even, pltpu.roll(odd, 64, 1))
    bottom = jnp.where(low, pltpu.roll(even, 64, 1), odd)
    return jnp.concatenate([top, bottom], axis=0).astype(bf16)


VMEM = pl.BlockSpec(memory_space=pltpu.VMEM)
HBM = pl.BlockSpec(memory_space=pltpu.HBM)
GROUP = 512
GROUPS = 4


def group_of(ref, group):
    return ref.at[:, pl.ds(GROUP * group, GROUP)]


def start_loading(cov_ref, held_ref, sems):
    copies = [
        pltpu.make_async_copy(group_of(cov_ref, g), held_ref.at[g], sems.at[g])
        for g in range(GROUPS)
    ]
    for copy in copies:
        copy.start()
    return copies


def params(mib):
    return pltpu.CompilerParams(vmem_limit_bytes=int(mib * 1048576))


def pack_kernel(first_ref, second_ref, out_ref, copies_ref):
    jac = jnp.concatenate([first_ref[...], second_ref[...]], axis=1)
    out_ref[...] = jac
    copies_ref[...] = jnp.broadcast_to(jac[None], (8, 32, 128))


def pack(first, second):
    return pl.pallas_call(
        pack_kernel,
        in_specs=[VMEM] * 2,
        out_specs=[VMEM] * 2,
        out_shape=[
            jax.ShapeDtypeStruct((32, 128), bf16),
            jax.ShapeDtypeStruct((8, 32, 128), bf16),
        ],
        compiler_params=params(4),
        name="pack",
    )(first, second)


EARLY = 3


def load_kernel(cov_ref, out_ref, sems):
    copies = [
        pltpu.make_async_copy(group_of(cov_ref, g), out_ref.at[g], sems.at[g])
        for g in range(EARLY)
    ]
    for copy in copies:
        copy.start()
    for copy in copies:
        copy.wait()


def load(cov):
    return pl.pallas_call(
        load_kernel,
        in_specs=[HBM],
        out_specs=VMEM,
        out_shape=jax.ShapeDtypeStruct((EARLY, 512, GROUP), f32),
        scratch_shapes=[pltpu.SemaphoreType.DMA((EARLY,))],
        compiler_params=params(16),
        name="load",
    )(cov)


def product_kernel(jac_ref, early_ref, cov_ref, out_ref, late_ref, sems):
    copies = [
        pltpu.make_async_copy(group_of(cov_ref, g), late_ref.at[g - EARLY], sems.at[g - EARLY])
        for g in range(EARLY, GROUPS)
    ]
    for copy in copies:
        copy.start()
    core = lax.rem(lax.axis_index("col"), 2)
    blocks = [paired(jac_ref[2 * q], jac_ref[2 * q + 1]) for q in range(4)]
    jac = jnp.concatenate(blocks, axis=1)
    dims = ((1,), (0,))
    for group in range(GROUPS):
        if group >= EARLY:
            copies[group - EARLY].wait()
        hi, low = halves(early_ref[group] if group < EARLY else late_ref[group - EARLY])
        part = dot(jac, low, dims) + dot(jac, hi, dims)
        for step in range(GROUP // 128):
            for h in range(2):
                place = piece_at(GROUP // 128 * group + step, h, core)
                out_ref[place] = part[32 * h : 32 * h + 32, 128 * step : 128 * step + 128]


def product(jac, early, cov):
    return pl.pallas_call(
        product_kernel,
        in_specs=[VMEM, VMEM, HBM],
        out_specs=VMEM,
        out_shape=jax.ShapeDtypeStruct((32, 32, 128), f32),
        scratch_shapes=[
            pltpu.VMEM((GROUPS - EARLY, 512, GROUP), f32),
            pltpu.SemaphoreType.DMA((GROUPS - EARLY,)),
        ],
        compiler_params=params(16),
        name="product",
    )(jac, early, cov)


def reduce_kernel(parts_ref, same_ref, other_ref, own_ref, kept_ref, sent_ref):
    total = jnp.sum(parts_ref[...], axis=0)
    own_ref[...] = total
    dims = ((1,), (1,))
    hi, mid, low = thirds(total)
    second = lax.rem(lax.axis_index("row"), 2) == 1
    same, other = same_ref[...].astype(f32), other_ref[...].astype(f32)
    jac = paired(jnp.where(second, other, same), jnp.where(second, same, other))
    gram = dot(jac, low, dims) + dot(jac, mid, dims) + dot(jac, hi, dims)
    packed = jnp.concatenate([gram[16 * q : 16 * q + 16] for q in range(4)], axis=1)
    first = lax.rem(lax.axis_index("col"), 2) == 0
    kept_ref[...] = jnp.where(first, packed[:8], packed[8:])
    sent_ref[...] = jnp.where(first, packed[8:], packed[:8])


def reduce(parts, same, other):
    return pl.pallas_call(
        reduce_kernel,
        in_specs=[VMEM] * 3,
        out_specs=[VMEM] * 3,
        out_shape=[
            jax.ShapeDtypeStruct((32, 128), f32),
            jax.ShapeDtypeStruct((8, 128), f32),
            jax.ShapeDtypeStruct((8, 128), f32),
        ],
        compiler_params=params(8),
        name="reduce",
    )(parts, same, other)


def fill_kernel(own_ref, kept_ref, got_ref, out_ref):
    out_ref[:, :32] = jnp.broadcast_to(own_ref[...][None], (32, 32, 128))
    gram = kept_ref[...] + got_ref[...]
    out_ref[:, 32:] = jnp.broadcast_to(gram[None], (32, 8, 128))


def fill(own, kept, got):
    return pl.pallas_call(
        fill_kernel,
        in_specs=[VMEM] * 3,
        out_specs=VMEM,
        out_shape=jax.ShapeDtypeStruct((32, 40, 128), f32),
        compiler_params=params(8),
        name="fill",
    )(own, kept, got)


def spread_kernel(parts_ref, natural_ref, out_ref):
    out_ref[:, :32] = jnp.broadcast_to(natural_ref[...][None], (8, 32, 128))
    for h in range(2):
        total = parts_ref[h, 32:]
        for t in range(1, 16):
            total = total + parts_ref[2 * t + h, 32:]
        out_ref[:, 32 + 8 * h : 40 + 8 * h] = jnp.broadcast_to(total[None], (8, 8, 128))


def spread(parts, natural):
    return pl.pallas_call(
        spread_kernel,
        in_specs=[VMEM] * 2,
        out_specs=VMEM,
        out_shape=jax.ShapeDtypeStruct((8, 48, 128), f32),
        compiler_params=params(4),
        name="spread",
    )(parts, natural)


PANEL = 8


def inverse_factor(first, second):
    left = jnp.concatenate([first[:, 32 * q : 32 * q + 32] for q in range(4)], axis=0)
    right = jnp.concatenate([second[:, 32 * q : 32 * q + 32] for q in range(4)], axis=0)
    gram = jnp.concatenate([left, right, jnp.zeros((64, 64), f32)], axis=1)
    rows = lax.broadcasted_iota(jnp.int32, (64, 128), 0)
    lanes = lax.broadcasted_iota(jnp.int32, (64, 128), 1)
    shift = jnp.where(rows < 32, lam_start, lam_start * lam_next).astype(f32)
    work = gram + jnp.where(rows == lanes, shift, 0.0) + jnp.where(rows + 64 == lanes, 1.0, 0.0)
    done = []
    for start in range(0, 64, PANEL):
        pivots = [work[j : j + 1, :] for j in range(PANEL)]
        rest = work[PANEL:, :]
        low = rest.shape[0]
        spots = range(start, start + PANEL)
        entry = {
            (i, j): jnp.broadcast_to(pivots[i][:, start + j : start + j + 1], (1, 128))
            for i in range(PANEL)
            for j in range(i + 1)
        }
        columns = [jnp.broadcast_to(rest[:, j : j + 1], (low, 128)) for j in spots] if low else []
        for j in range(PANEL):
            inverse = 1.0 / entry[j, j]
            factors = {i: entry[i, j] * inverse for i in range(j + 1, PANEL)}
            for i in range(j + 1, PANEL):
                pivots[i] = pivots[i] - factors[i] * pivots[j]
                for m in range(j + 1, i + 1):
                    entry[i, m] = entry[i, m] - factors[m] * entry[i, j]
                if low:
                    columns[i] = columns[i] - factors[i] * columns[j]
            done.append(pivots[j] * lax.rsqrt(entry[j, j]))
            if low:
                rest = rest - columns[j] * (pivots[j] * inverse)
        work = rest
    return jnp.concatenate(done, axis=0)[:, 64:]


def update_kernel(
    cov_ref, cols_ref, rows_ref, first_ref, second_ref, out_ref, inc_ref, held_ref, in_sems, out_sems
):
    loads = start_loading(cov_ref, held_ref, in_sems)
    col = lax.axis_index("col")
    core = lax.rem(col, 2)
    first, second = [
        jnp.concatenate(
            [
                sum(rows_ref[2 * y + k, 32 + 8 * h : 40 + 8 * h] for y in range(1, 4))
                + rows_ref[k, 32 + 8 * h : 40 + 8 * h]
                for k in range(2)
            ],
            axis=0,
        )
        for h in range(2)
    ]
    inverse = inverse_factor(first, second)
    hi, mid, low = thirds(inverse)
    inverse_parts = jnp.concatenate([hi, hi, hi, mid, mid, low], axis=1)

    def whitened(block):
        hi, mid, low = thirds(block)
        parts = jnp.concatenate([hi, mid, low, hi, mid, hi], axis=0)
        return dot(inverse_parts, parts, ((1,), (0,)))

    rows = whitened(
        jnp.concatenate(
            [
                jnp.concatenate([rows_ref[2 * t, :32], rows_ref[2 * t + 1, :32]], axis=0)
                for t in range(4)
            ],
            axis=1,
        )
    )
    hi, low = halves(rows.T)
    left = jnp.concatenate([hi, hi, low, low], axis=1)
    errors = jnp.concatenate([first_ref[...], second_ref[...]], axis=1)
    weights = jnp.sum(inverse * errors, axis=1, keepdims=True)
    inc = jnp.sum(rows * weights, axis=0, keepdims=True)
    own = jnp.zeros((1, 128), f32)
    for tile in range(4):
        own = own + jnp.where(col // 2 == tile, inc[:, 128 * tile : 128 * tile + 128], 0.0)
    inc_ref[...] = jnp.where(core == 1, own[:, 64:], own[:, :64])

    cols = whitened(
        jnp.concatenate(
            [
                jnp.concatenate([cols_ref[piece_at(tile, h, core), :32] for h in range(2)], axis=0)
                for tile in range(16)
            ],
            axis=1,
        )
    )
    hi, low = halves(cols)
    right = jnp.concatenate([hi, low, hi, low], axis=0)
    for load in loads:
        load.wait()
    stores = []
    for group in range(GROUPS):
        change = dot(left, right[:, GROUP * group : GROUP * group + GROUP], ((1,), (0,)))
        held_ref[group] = (held_ref[group] - change) * (1.0 / (lam_start * lam_next))
        store = pltpu.make_async_copy(
            held_ref.at[group], group_of(out_ref, group), out_sems.at[group]
        )
        store.start()
        stores.append(store)
    for store in stores:
        store.wait()


def update(cov, cols, rows, first, second):
    return pl.pallas_call(
        update_kernel,
        in_specs=[HBM] + [VMEM] * 4,
        out_specs=[HBM, VMEM],
        out_shape=[
            jax.ShapeDtypeStruct((512, 2048), f32),
            jax.ShapeDtypeStruct((1, 64), f32),
        ],
        scratch_shapes=[
            pltpu.VMEM((GROUPS, 512, GROUP), f32),
            pltpu.SemaphoreType.DMA((GROUPS,)),
            pltpu.SemaphoreType.DMA((GROUPS,)),
        ],
        compiler_params=params(16),
        name="update",
    )(cov, cols, rows, first, second)


def exchange(array, axis):
    return lax.all_to_all(array, axis, 0, 0, tiled=True)


def body(covariance, first_jacobian, second_jacobian, first_residuals, second_residuals):
    both = ("row", "col")
    covariance, first_jacobian, second_jacobian = [
        pltpu.with_memory_space_constraint(array, pltpu.HBM)
        for array in (covariance, first_jacobian, second_jacobian)
    ]
    jac, jac_copies = pack(first_jacobian, second_jacobian)
    jac_rows = exchange(jac_copies, "col")
    same = lax.ppermute(jac, both, reversed_pairs(to_row_block(0)))
    other = lax.ppermute(jac, both, reversed_pairs(to_row_block(1)))
    held = load(covariance)
    parts = product(jac_rows, held, covariance)
    parts = exchange(parts, "row")
    own, kept, sent = reduce(parts, same, other)
    got = lax.ppermute(sent, "col", [(c, c ^ 1) for c in range(8)])
    cols = exchange(fill(own, kept, got), "row")
    natural = lax.ppermute(own, both, to_row_block(0))
    rows = exchange(spread(cols, natural), "col")
    out, increment = update(covariance, cols, rows, first_residuals[None], second_residuals[None])
    return out, increment[0]


def solution(mesh):
    return jax.shard_map(
        body,
        mesh=mesh,
        in_specs=(P("row", "col"), P(None, ("row", "col")), P(None, ("row", "col")), P(), P()),
        out_specs=(P("row", "col"), P(("row", "col"))),
        check_vma=False,
    )
```

```python
import jax
import jax.numpy as jnp
from jax import lax
from jax.experimental import pallas as pl
from jax.experimental.pallas import tpu as pltpu
from jax.sharding import PartitionSpec as P


lam_start = 0.98
forget_rate = 0.9987
lam_next = forget_rate * lam_start + (1.0 - forget_rate)

f32 = jnp.float32
bf16 = jnp.bfloat16


def device(x, y, z, k):
    return (x * 8 + z) * 8 + y * 2 + k


def to_row_block():
    pairs = []
    for x in range(4):
        for y in range(4):
            for z in range(8):
                for k in range(2):
                    i = ((z + 2 + 4 * k) % 8) // 2
                    target = device(y, (x + 2) % 4, 4 * k + i, z % 2)
                    pairs.append((device(x, y, z, k), target))
    return pairs


def reversed_pairs(pairs):
    return [(b, a) for a, b in pairs]


def piece_at(tile, h, core):
    return (tile % 4 + 2) % 4, lax.rem(2 * (tile // 4) + h + 6 + 4 * core, 8)


def halves(value):
    hi = value.astype(bf16)
    return hi, (value - hi.astype(f32)).astype(bf16)


def thirds(value):
    hi = value.astype(bf16)
    rest = value - hi.astype(f32)
    mid = rest.astype(bf16)
    return hi, mid, (rest - mid.astype(f32)).astype(bf16)


def dot(a, b, dims):
    return lax.dot_general(a, b, (dims, ((), ())), preferred_element_type=f32)


def paired(even, odd):
    even, odd = even.astype(f32), odd.astype(f32)
    low = lax.broadcasted_iota(jnp.int32, even.shape, 1) < 64
    top = jnp.where(low, even, pltpu.roll(odd, 64, 1))
    bottom = jnp.where(low, pltpu.roll(even, 64, 1), odd)
    return jnp.concatenate([top, bottom], axis=0).astype(bf16)


VMEM = pl.BlockSpec(memory_space=pltpu.VMEM)
HBM = pl.BlockSpec(memory_space=pltpu.HBM)
GROUP = 512
GROUPS = 4


def group_of(ref, group):
    return ref.at[:, pl.ds(GROUP * group, GROUP)]


def start_loading(cov_ref, held_ref, sems):
    copies = [
        pltpu.make_async_copy(group_of(cov_ref, g), held_ref.at[g], sems.at[g])
        for g in range(GROUPS)
    ]
    for copy in copies:
        copy.start()
    return copies


def params(mib):
    return pltpu.CompilerParams(vmem_limit_bytes=int(mib * 1048576))


EARLY = 3


def load_kernel(cov_ref, out_ref, sems):
    copies = [
        pltpu.make_async_copy(group_of(cov_ref, g), out_ref.at[g], sems.at[g])
        for g in range(EARLY)
    ]
    for copy in copies:
        copy.start()
    for copy in copies:
        copy.wait()


def load(cov):
    return pl.pallas_call(
        load_kernel,
        in_specs=[HBM],
        out_specs=VMEM,
        out_shape=jax.ShapeDtypeStruct((EARLY, 512, GROUP), f32),
        scratch_shapes=[pltpu.SemaphoreType.DMA((EARLY,))],
        compiler_params=params(16),
        name="load",
    )(cov)


def product_kernel(jac_ref, early_ref, cov_ref, out_ref, own_ref, late_ref, sems):
    copies = [
        pltpu.make_async_copy(group_of(cov_ref, g), late_ref.at[g - EARLY], sems.at[g - EARLY])
        for g in range(EARLY, GROUPS)
    ]
    for copy in copies:
        copy.start()
    col = lax.axis_index("col")
    core = lax.rem(col, 2)
    blocks = [paired(jac_ref[2 * q], jac_ref[2 * q + 1]) for q in range(4)]
    own = blocks[0]
    for q in range(1, 4):
        own = jnp.where(col // 2 == q, blocks[q], own)
    own_ref[...] = own
    jac = jnp.concatenate(blocks, axis=1)
    dims = ((1,), (0,))
    for group in range(GROUPS):
        if group >= EARLY:
            copies[group - EARLY].wait()
        hi, low = halves(early_ref[group] if group < EARLY else late_ref[group - EARLY])
        part = dot(jac, low, dims) + dot(jac, hi, dims)
        for step in range(GROUP // 128):
            for h in range(2):
                x, z = piece_at(GROUP // 128 * group + step, h, core)
                out_ref[x * 8 + z] = part[32 * h : 32 * h + 32, 128 * step : 128 * step + 128]


def product(jac, early, cov):
    return pl.pallas_call(
        product_kernel,
        in_specs=[VMEM, VMEM, HBM],
        out_specs=[VMEM] * 2,
        out_shape=[
            jax.ShapeDtypeStruct((32, 32, 128), f32),
            jax.ShapeDtypeStruct((64, 128), bf16),
        ],
        scratch_shapes=[
            pltpu.VMEM((GROUPS - EARLY, 512, GROUP), f32),
            pltpu.SemaphoreType.DMA((GROUPS - EARLY,)),
        ],
        compiler_params=params(16),
        name="product",
    )(jac, early, cov)


def reduce_kernel(parts_ref, jac_ref, own_ref, line_ref):
    total = jnp.sum(parts_ref[...], axis=0)
    own_ref[...] = total
    dims = ((1,), (1,))
    hi, mid, low = thirds(total)
    jac = jac_ref[...]
    gram = dot(jac, low, dims) + dot(jac, mid, dims) + dot(jac, hi, dims)
    packed = jnp.concatenate([gram[16 * q : 16 * q + 16] for q in range(4)], axis=1)
    line_ref[:, :32] = jnp.broadcast_to(total[None], (8, 32, 128))
    line_ref[:, 32:] = jnp.broadcast_to(packed[None], (8, 16, 128))


def reduce(parts, jac):
    return pl.pallas_call(
        reduce_kernel,
        in_specs=[VMEM] * 2,
        out_specs=[VMEM] * 2,
        out_shape=[
            jax.ShapeDtypeStruct((32, 128), f32),
            jax.ShapeDtypeStruct((8, 48, 128), f32),
        ],
        compiler_params=params(8),
        name="reduce",
    )(parts, jac)


def spread_kernel(parts_ref, natural_ref, line_ref, out_ref):
    line_ref[...] = parts_ref[:, :32]
    out_ref[:, :32] = jnp.broadcast_to(natural_ref[...][None], (8, 32, 128))
    for h in range(2):
        total = parts_ref[h, 32:]
        for z in range(h + 2, 8, 2):
            total = total + parts_ref[z, 32:]
        out_ref[:, 32 + 16 * h : 48 + 16 * h] = jnp.broadcast_to(total[None], (8, 16, 128))


def spread(parts, natural):
    return pl.pallas_call(
        spread_kernel,
        in_specs=[VMEM] * 2,
        out_specs=[VMEM] * 2,
        out_shape=[
            jax.ShapeDtypeStruct((8, 32, 128), f32),
            jax.ShapeDtypeStruct((8, 64, 128), f32),
        ],
        compiler_params=params(4),
        name="spread",
    )(parts, natural)


def gather_kernel(rows_ref, out_ref):
    total = rows_ref[0, 32:]
    for c in range(1, 8):
        total = total + rows_ref[c, 32:]
    out_ref[...] = total


def gather(rows):
    return pl.pallas_call(
        gather_kernel,
        in_specs=[VMEM],
        out_specs=VMEM,
        out_shape=jax.ShapeDtypeStruct((32, 128), f32),
        compiler_params=params(4),
        name="gather",
    )(rows)


PANEL = 8


def inverse_factor(first, second):
    left = jnp.concatenate([first[:, 32 * q : 32 * q + 32] for q in range(4)], axis=0)
    right = jnp.concatenate([second[:, 32 * q : 32 * q + 32] for q in range(4)], axis=0)
    gram = jnp.concatenate([left, right, jnp.zeros((64, 64), f32)], axis=1)
    rows = lax.broadcasted_iota(jnp.int32, (64, 128), 0)
    lanes = lax.broadcasted_iota(jnp.int32, (64, 128), 1)
    shift = jnp.where(rows < 32, lam_start, lam_start * lam_next).astype(f32)
    work = gram + jnp.where(rows == lanes, shift, 0.0) + jnp.where(rows + 64 == lanes, 1.0, 0.0)
    done = []
    for start in range(0, 64, PANEL):
        pivots = [work[j : j + 1, :] for j in range(PANEL)]
        rest = work[PANEL:, :]
        low = rest.shape[0]
        spots = range(start, start + PANEL)
        entry = {
            (i, j): jnp.broadcast_to(pivots[i][:, start + j : start + j + 1], (1, 128))
            for i in range(PANEL)
            for j in range(i + 1)
        }
        columns = [jnp.broadcast_to(rest[:, j : j + 1], (low, 128)) for j in spots] if low else []
        for j in range(PANEL):
            inverse = 1.0 / entry[j, j]
            factors = {i: entry[i, j] * inverse for i in range(j + 1, PANEL)}
            for i in range(j + 1, PANEL):
                pivots[i] = pivots[i] - factors[i] * pivots[j]
                for m in range(j + 1, i + 1):
                    entry[i, m] = entry[i, m] - factors[m] * entry[i, j]
                if low:
                    columns[i] = columns[i] - factors[i] * columns[j]
            done.append(pivots[j] * lax.rsqrt(entry[j, j]))
            if low:
                rest = rest - columns[j] * (pivots[j] * inverse)
        work = rest
    return jnp.concatenate(done, axis=0)[:, 64:]


def update_kernel(
    cov_ref,
    line_refs,
    gram_refs,
    rows_ref,
    first_ref,
    second_ref,
    out_ref,
    inc_ref,
    held_ref,
    cols_ref,
    in_sems,
    out_sems,
):
    loads = start_loading(cov_ref, held_ref, in_sems)
    col = lax.axis_index("col")
    core = lax.rem(col, 2)
    x = lax.axis_index("row") // 8
    for turn, line_ref in enumerate(line_refs):
        cols_ref[lax.rem(x + turn, 4)] = line_ref[...]
    total = (gram_refs[0][...] + gram_refs[1][...]) + (gram_refs[2][...] + gram_refs[3][...])
    first, second = total[:16], total[16:]
    inverse = inverse_factor(first, second)
    hi, mid, low = thirds(inverse)
    inverse_parts = jnp.concatenate([hi, hi, hi, mid, mid, low], axis=1)

    def whitened(block):
        hi, mid, low = thirds(block)
        parts = jnp.concatenate([hi, mid, low, hi, mid, hi], axis=0)
        return dot(inverse_parts, parts, ((1,), (0,)))

    rows = whitened(
        jnp.concatenate(
            [
                jnp.concatenate([rows_ref[2 * t, :32], rows_ref[2 * t + 1, :32]], axis=0)
                for t in range(4)
            ],
            axis=1,
        )
    )
    hi, low = halves(rows.T)
    left = jnp.concatenate([hi, hi, low, low], axis=1)
    errors = jnp.concatenate([first_ref[...], second_ref[...]], axis=1)
    weights = jnp.sum(inverse * errors, axis=1, keepdims=True)
    inc = jnp.sum(rows * weights, axis=0, keepdims=True)
    own = jnp.zeros((1, 128), f32)
    for tile in range(4):
        own = own + jnp.where(col // 2 == tile, inc[:, 128 * tile : 128 * tile + 128], 0.0)
    inc_ref[...] = jnp.where(core == 1, own[:, 64:], own[:, :64])

    cols = whitened(
        jnp.concatenate(
            [
                jnp.concatenate([cols_ref[piece_at(tile, h, core)] for h in range(2)], axis=0)
                for tile in range(16)
            ],
            axis=1,
        )
    )
    hi, low = halves(cols)
    right = jnp.concatenate([hi, low, hi, low], axis=0)
    for load in loads:
        load.wait()
    stores = []
    for group in range(GROUPS):
        change = dot(left, right[:, GROUP * group : GROUP * group + GROUP], ((1,), (0,)))
        held_ref[group] = (held_ref[group] - change) * (1.0 / (lam_start * lam_next))
        store = pltpu.make_async_copy(
            held_ref.at[group], group_of(out_ref, group), out_sems.at[group]
        )
        store.start()
        stores.append(store)
    for store in stores:
        store.wait()


def update(cov, lines, grams, rows, first, second):
    return pl.pallas_call(
        update_kernel,
        in_specs=[HBM, [VMEM] * 4, [VMEM] * 4] + [VMEM] * 3,
        out_specs=[HBM, VMEM],
        out_shape=[
            jax.ShapeDtypeStruct((512, 2048), f32),
            jax.ShapeDtypeStruct((1, 64), f32),
        ],
        scratch_shapes=[
            pltpu.VMEM((GROUPS, 512, GROUP), f32),
            pltpu.VMEM((4, 8, 32, 128), f32),
            pltpu.SemaphoreType.DMA((GROUPS,)),
            pltpu.SemaphoreType.DMA((GROUPS,)),
        ],
        compiler_params=params(16),
        name="update",
    )(cov, lines, grams, rows, first, second)


def exchange(array, axis, groups=None):
    return lax.all_to_all(array, axis, 0, 0, axis_index_groups=groups, tiled=True)


Z_LINES = [[8 * x + z for z in range(8)] for x in range(4)]


def along_x(array):
    def at(turn):
        pairs = [((r + 8 * turn) % 32, r) for r in range(32)]
        return lax.ppermute(array, "row", pairs)

    return [array] + [at(turn) for turn in (1, 2, 3)]


def body(covariance, first_jacobian, second_jacobian, first_residuals, second_residuals):
    both = ("row", "col")
    jac = jnp.concatenate([first_jacobian, second_jacobian], axis=1)
    jac_rows = exchange(jnp.broadcast_to(jac[None], (8, 32, 128)), "col")
    covariance = pltpu.with_memory_space_constraint(covariance, pltpu.HBM)
    held = load(covariance)
    parts, jac_own = product(jac_rows, held, covariance)
    parts = exchange(parts, "row")
    jac_piece = lax.ppermute(jac_own, both, reversed_pairs(to_row_block()))
    own, line = reduce(parts, jac_piece)
    line = exchange(line, "row", Z_LINES)
    natural = lax.ppermute(own, both, to_row_block())
    line, rows = spread(line, natural)
    rows = exchange(rows, "col")
    lines = along_x(line)
    grams = along_x(gather(rows))
    out, increment = update(
        covariance, lines, grams, rows, first_residuals[None], second_residuals[None]
    )
    return out, increment[0]


def solution(mesh):
    return jax.shard_map(
        body,
        mesh=mesh,
        in_specs=(P("row", "col"), P(None, ("row", "col")), P(None, ("row", "col")), P(), P()),
        out_specs=(P("row", "col"), P(("row", "col"))),
        check_vma=False,
    )
```

```python
import jax
import jax.numpy as jnp
from jax import lax
from jax.experimental import pallas as pl
from jax.experimental.pallas import tpu as pltpu
from jax.sharding import PartitionSpec as P


lam_start = 0.98
forget_rate = 0.9987
lam_next = forget_rate * lam_start + (1.0 - forget_rate)

f32 = jnp.float32
bf16 = jnp.bfloat16


def device(x, y, z, k):
    return (x * 8 + z) * 8 + y * 2 + k


def to_row_block():
    pairs = []
    for x in range(4):
        for y in range(4):
            for z in range(8):
                for k in range(2):
                    i = ((z + 2 + 4 * k) % 8) // 2
                    target = device(y, (x + 2) % 4, 4 * k + i, z % 2)
                    pairs.append((device(x, y, z, k), target))
    return pairs


def reversed_pairs(pairs):
    return [(b, a) for a, b in pairs]


def piece_at(tile, h, core):
    return (tile % 4 + 2) % 4, lax.rem(2 * (tile // 4) + h + 6 + 4 * core, 8)


def halves(value):
    hi = value.astype(bf16)
    return hi, (value - hi.astype(f32)).astype(bf16)


def thirds(value):
    hi = value.astype(bf16)
    rest = value - hi.astype(f32)
    mid = rest.astype(bf16)
    return hi, mid, (rest - mid.astype(f32)).astype(bf16)


def dot(a, b, dims):
    return lax.dot_general(a, b, (dims, ((), ())), preferred_element_type=f32)


def paired(even, odd):
    even, odd = even.astype(f32), odd.astype(f32)
    low = lax.broadcasted_iota(jnp.int32, even.shape, 1) < 64
    top = jnp.where(low, even, pltpu.roll(odd, 64, 1))
    bottom = jnp.where(low, pltpu.roll(even, 64, 1), odd)
    return jnp.concatenate([top, bottom], axis=0).astype(bf16)


VMEM = pl.BlockSpec(memory_space=pltpu.VMEM)
HBM = pl.BlockSpec(memory_space=pltpu.HBM)
GROUP = 512
GROUPS = 4


def group_of(ref, group):
    return ref.at[:, pl.ds(GROUP * group, GROUP)]


def start_loading(cov_ref, held_ref, sems, first):
    copies = [
        pltpu.make_async_copy(group_of(cov_ref, g), held_ref.at[g], sems.at[g])
        for g in range(first, GROUPS)
    ]
    for copy in copies:
        copy.start()
    return copies


def params(mib):
    return pltpu.CompilerParams(vmem_limit_bytes=int(mib * 1048576))


def load(cov, count):
    def load_kernel(cov_ref, out_ref, sems):
        copies = [
            pltpu.make_async_copy(group_of(cov_ref, g), out_ref.at[g], sems.at[g])
            for g in range(count)
        ]
        for copy in copies:
            copy.start()
        for copy in copies:
            copy.wait()

    return pl.pallas_call(
        load_kernel,
        in_specs=[HBM],
        out_specs=VMEM,
        out_shape=jax.ShapeDtypeStruct((count, 512, GROUP), f32),
        scratch_shapes=[pltpu.SemaphoreType.DMA((count,))],
        compiler_params=params(16),
        name="fetch",
    )(cov)


EARLY = 3
AGAIN = 2


def product_kernel(jac_ref, early_ref, cov_ref, out_refs, own_ref, late_ref, whole_ref, sems):
    copies = [
        pltpu.make_async_copy(group_of(cov_ref, g), late_ref.at[g - EARLY], sems.at[g - EARLY])
        for g in range(EARLY, GROUPS)
    ]
    for copy in copies:
        copy.start()
    col = lax.axis_index("col")
    core = lax.rem(col, 2)
    blocks = [paired(jac_ref[2 * q], jac_ref[2 * q + 1]) for q in range(4)]
    own = blocks[0]
    for q in range(1, 4):
        own = jnp.where(col // 2 == q, blocks[q], own)
    own_ref[...] = own
    jac = jnp.concatenate(blocks, axis=1)
    dims = ((1,), (0,))
    for group in range(GROUPS):
        if group >= EARLY:
            copies[group - EARLY].wait()
        hi, low = halves(early_ref[group] if group < EARLY else late_ref[group - EARLY])
        part = dot(jac, low, dims) + dot(jac, hi, dims)
        for step in range(GROUP // 128):
            for h in range(2):
                x, z = piece_at(GROUP // 128 * group + step, h, core)
                whole_ref[x, z] = part[32 * h : 32 * h + 32, 128 * step : 128 * step + 128]
    x = lax.axis_index("row") // 8
    for turn in range(4):
        out_refs[turn][...] = whole_ref[lax.rem(x + turn, 4)]


def product(jac, early, cov):
    return pl.pallas_call(
        product_kernel,
        in_specs=[VMEM, VMEM, HBM],
        out_specs=[[VMEM] * 4, VMEM],
        out_shape=[
            [jax.ShapeDtypeStruct((8, 32, 128), f32)] * 4,
            jax.ShapeDtypeStruct((64, 128), bf16),
        ],
        scratch_shapes=[
            pltpu.VMEM((GROUPS - EARLY, 512, GROUP), f32),
            pltpu.VMEM((4, 8, 32, 128), f32),
            pltpu.SemaphoreType.DMA((GROUPS - EARLY,)),
        ],
        compiler_params=params(16),
        name="product",
    )(jac, early, cov)


def add_kernel(first_ref, second_ref, third_ref, fourth_ref, out_ref):
    out_ref[...] = (first_ref[...] + second_ref[...]) + (third_ref[...] + fourth_ref[...])


def add(parts):
    return pl.pallas_call(
        add_kernel,
        in_specs=[VMEM] * 4,
        out_specs=VMEM,
        out_shape=jax.ShapeDtypeStruct((8, 32, 128), f32),
        compiler_params=params(8),
        name="add",
    )(*parts)


def reduce_kernel(parts_ref, jac_ref, own_ref, line_ref):
    total = jnp.sum(parts_ref[...], axis=0)
    own_ref[...] = total
    dims = ((1,), (1,))
    hi, mid, low = thirds(total)
    jac = jac_ref[...]
    gram = dot(jac, low, dims) + dot(jac, mid, dims) + dot(jac, hi, dims)
    packed = jnp.concatenate([gram[16 * q : 16 * q + 16] for q in range(4)], axis=1)
    line_ref[:, :32] = jnp.broadcast_to(total[None], (8, 32, 128))
    line_ref[:, 32:] = jnp.broadcast_to(packed[None], (8, 16, 128))


def reduce(parts, jac):
    return pl.pallas_call(
        reduce_kernel,
        in_specs=[VMEM] * 2,
        out_specs=[VMEM] * 2,
        out_shape=[
            jax.ShapeDtypeStruct((32, 128), f32),
            jax.ShapeDtypeStruct((8, 48, 128), f32),
        ],
        compiler_params=params(8),
        name="reduce",
    )(parts, jac)


def spread_kernel(parts_ref, natural_ref, line_ref, out_ref):
    line_ref[...] = parts_ref[:, :32]
    out_ref[:, :32] = jnp.broadcast_to(natural_ref[...][None], (8, 32, 128))
    for h in range(2):
        total = parts_ref[h, 32:]
        for z in range(h + 2, 8, 2):
            total = total + parts_ref[z, 32:]
        out_ref[:, 32 + 16 * h : 48 + 16 * h] = jnp.broadcast_to(total[None], (8, 16, 128))


def spread(parts, natural):
    return pl.pallas_call(
        spread_kernel,
        in_specs=[VMEM] * 2,
        out_specs=[VMEM] * 2,
        out_shape=[
            jax.ShapeDtypeStruct((8, 32, 128), f32),
            jax.ShapeDtypeStruct((8, 64, 128), f32),
        ],
        compiler_params=params(4),
        name="spread",
    )(parts, natural)


def gather_kernel(rows_ref, out_ref):
    total = rows_ref[0, 32:]
    for c in range(1, 8):
        total = total + rows_ref[c, 32:]
    out_ref[...] = total


def gather(rows):
    return pl.pallas_call(
        gather_kernel,
        in_specs=[VMEM],
        out_specs=VMEM,
        out_shape=jax.ShapeDtypeStruct((32, 128), f32),
        compiler_params=params(4),
        name="gather",
    )(rows)


PANEL = 8


def inverse_factor(first, second):
    left = jnp.concatenate([first[:, 32 * q : 32 * q + 32] for q in range(4)], axis=0)
    right = jnp.concatenate([second[:, 32 * q : 32 * q + 32] for q in range(4)], axis=0)
    gram = jnp.concatenate([left, right, jnp.zeros((64, 64), f32)], axis=1)
    rows = lax.broadcasted_iota(jnp.int32, (64, 128), 0)
    lanes = lax.broadcasted_iota(jnp.int32, (64, 128), 1)
    shift = jnp.where(rows < 32, lam_start, lam_start * lam_next).astype(f32)
    work = gram + jnp.where(rows == lanes, shift, 0.0) + jnp.where(rows + 64 == lanes, 1.0, 0.0)
    done = []
    for start in range(0, 64, PANEL):
        pivots = [work[j : j + 1, :] for j in range(PANEL)]
        rest = work[PANEL:, :]
        low = rest.shape[0]
        spots = range(start, start + PANEL)
        entry = {
            (i, j): jnp.broadcast_to(pivots[i][:, start + j : start + j + 1], (1, 128))
            for i in range(PANEL)
            for j in range(i + 1)
        }
        columns = [jnp.broadcast_to(rest[:, j : j + 1], (low, 128)) for j in spots] if low else []
        for j in range(PANEL):
            inverse = 1.0 / entry[j, j]
            factors = {i: entry[i, j] * inverse for i in range(j + 1, PANEL)}
            for i in range(j + 1, PANEL):
                pivots[i] = pivots[i] - factors[i] * pivots[j]
                for m in range(j + 1, i + 1):
                    entry[i, m] = entry[i, m] - factors[m] * entry[i, j]
                if low:
                    columns[i] = columns[i] - factors[i] * columns[j]
            done.append(pivots[j] * lax.rsqrt(entry[j, j]))
            if low:
                rest = rest - columns[j] * (pivots[j] * inverse)
        work = rest
    return jnp.concatenate(done, axis=0)[:, 64:]


def update_kernel(
    early_ref,
    cov_ref,
    line_refs,
    gram_refs,
    rows_ref,
    first_ref,
    second_ref,
    out_ref,
    inc_ref,
    held_ref,
    cols_ref,
    in_sems,
    out_sems,
):
    loads = start_loading(cov_ref, held_ref, in_sems, AGAIN)
    col = lax.axis_index("col")
    core = lax.rem(col, 2)
    x = lax.axis_index("row") // 8
    for turn, line_ref in enumerate(line_refs):
        cols_ref[lax.rem(x + turn, 4)] = line_ref[...]
    total = (gram_refs[0][...] + gram_refs[1][...]) + (gram_refs[2][...] + gram_refs[3][...])
    first, second = total[:16], total[16:]
    inverse = inverse_factor(first, second)
    hi, mid, low = thirds(inverse)
    inverse_parts = jnp.concatenate([hi, hi, hi, mid, mid, low], axis=1)

    def whitened(block):
        hi, mid, low = thirds(block)
        parts = jnp.concatenate([hi, mid, low, hi, mid, hi], axis=0)
        return dot(inverse_parts, parts, ((1,), (0,)))

    rows = whitened(
        jnp.concatenate(
            [
                jnp.concatenate([rows_ref[2 * t, :32], rows_ref[2 * t + 1, :32]], axis=0)
                for t in range(4)
            ],
            axis=1,
        )
    )
    hi, low = halves(rows.T)
    left = jnp.concatenate([hi, hi, low, low], axis=1)
    errors = jnp.concatenate([first_ref[...], second_ref[...]], axis=1)
    weights = jnp.sum(inverse * errors, axis=1, keepdims=True)
    inc = jnp.sum(rows * weights, axis=0, keepdims=True)
    own = jnp.zeros((1, 128), f32)
    for tile in range(4):
        own = own + jnp.where(col // 2 == tile, inc[:, 128 * tile : 128 * tile + 128], 0.0)
    inc_ref[...] = jnp.where(core == 1, own[:, 64:], own[:, :64])

    cols = whitened(
        jnp.concatenate(
            [
                jnp.concatenate([cols_ref[piece_at(tile, h, core)] for h in range(2)], axis=0)
                for tile in range(16)
            ],
            axis=1,
        )
    )
    hi, low = halves(cols)
    right = jnp.concatenate([hi, low, hi, low], axis=0)
    stores = []
    for group in range(GROUPS):
        change = dot(left, right[:, GROUP * group : GROUP * group + GROUP], ((1,), (0,)))
        if group >= AGAIN:
            loads[group - AGAIN].wait()
        old = early_ref[group] if group < AGAIN else held_ref[group]
        held_ref[group] = (old - change) * (1.0 / (lam_start * lam_next))
        store = pltpu.make_async_copy(
            held_ref.at[group], group_of(out_ref, group), out_sems.at[group]
        )
        store.start()
        stores.append(store)
    for store in stores:
        store.wait()


def update(early, cov, lines, grams, rows, first, second):
    return pl.pallas_call(
        update_kernel,
        in_specs=[VMEM, HBM, [VMEM] * 4, [VMEM] * 4] + [VMEM] * 3,
        out_specs=[HBM, VMEM],
        out_shape=[
            jax.ShapeDtypeStruct((512, 2048), f32),
            jax.ShapeDtypeStruct((1, 64), f32),
        ],
        scratch_shapes=[
            pltpu.VMEM((GROUPS, 512, GROUP), f32),
            pltpu.VMEM((4, 8, 32, 128), f32),
            pltpu.SemaphoreType.DMA((GROUPS,)),
            pltpu.SemaphoreType.DMA((GROUPS,)),
        ],
        compiler_params=params(16),
        name="update",
    )(early, cov, lines, grams, rows, first, second)


def exchange(array, axis, groups=None):
    return lax.all_to_all(array, axis, 0, 0, axis_index_groups=groups, tiled=True)


Z_LINES = [[8 * x + z for z in range(8)] for x in range(4)]


def moved(array, turn):
    return lax.ppermute(array, "row", [(r, (r + 8 * turn) % 32) for r in range(32)])


def along_x(array):
    return [array] + [moved(array, 4 - turn) for turn in (1, 2, 3)]


def body(covariance, first_jacobian, second_jacobian, first_residuals, second_residuals):
    both = ("row", "col")
    jac = jnp.concatenate([first_jacobian, second_jacobian], axis=1)
    jac_rows = exchange(jnp.broadcast_to(jac[None], (8, 32, 128)), "col")
    covariance = pltpu.with_memory_space_constraint(covariance, pltpu.HBM)
    held = load(covariance, EARLY)
    parts, jac_own = product(jac_rows, held, covariance)
    parts = parts[:1] + [moved(parts[turn], turn) for turn in (1, 2, 3)]
    parts = add(parts)
    parts = exchange(parts, "row", Z_LINES)
    jac_piece = lax.ppermute(jac_own, both, reversed_pairs(to_row_block()))
    own, line = reduce(parts, jac_piece)
    line = exchange(line, "row", Z_LINES)
    natural = lax.ppermute(own, both, to_row_block())
    line, rows = spread(line, natural)
    rows = exchange(rows, "col")
    lines = along_x(line)
    held = load(covariance, AGAIN)
    grams = along_x(gather(rows))
    out, increment = update(
        held, covariance, lines, grams, rows, first_residuals[None], second_residuals[None]
    )
    return out, increment[0]


def solution(mesh):
    return jax.shard_map(
        body,
        mesh=mesh,
        in_specs=(P("row", "col"), P(None, ("row", "col")), P(None, ("row", "col")), P(), P()),
        out_specs=(P("row", "col"), P(("row", "col"))),
        check_vma=False,
    )
```

```python
import jax
import jax.numpy as jnp
from jax import lax
from jax.experimental import pallas as pl
from jax.experimental.pallas import tpu as pltpu
from jax.sharding import PartitionSpec as P


lam_start = 0.98
forget_rate = 0.9987
lam_next = forget_rate * lam_start + (1.0 - forget_rate)

f32 = jnp.float32
bf16 = jnp.bfloat16


def device(x, y, z, k):
    return (x * 8 + z) * 8 + y * 2 + k


def to_row_block():
    pairs = []
    for x in range(4):
        for y in range(4):
            for z in range(8):
                for k in range(2):
                    i = ((z + 2 + 4 * k) % 8) // 2
                    target = device(y, (x + 2) % 4, 4 * k + i, z % 2)
                    pairs.append((device(x, y, z, k), target))
    return pairs


def reversed_pairs(pairs):
    return [(b, a) for a, b in pairs]


def piece_at(tile, h, core):
    return (tile % 4 + 2) % 4, lax.rem(2 * (tile // 4) + h + 6 + 4 * core, 8)


def halves(value):
    hi = value.astype(bf16)
    return hi, (value - hi.astype(f32)).astype(bf16)


def thirds(value):
    hi = value.astype(bf16)
    rest = value - hi.astype(f32)
    mid = rest.astype(bf16)
    return hi, mid, (rest - mid.astype(f32)).astype(bf16)


def dot(a, b, dims):
    return lax.dot_general(a, b, (dims, ((), ())), preferred_element_type=f32)


def paired(even, odd):
    even, odd = even.astype(f32), odd.astype(f32)
    low = lax.broadcasted_iota(jnp.int32, even.shape, 1) < 64
    top = jnp.where(low, even, pltpu.roll(odd, 64, 1))
    bottom = jnp.where(low, pltpu.roll(even, 64, 1), odd)
    return jnp.concatenate([top, bottom], axis=0).astype(bf16)


VMEM = pl.BlockSpec(memory_space=pltpu.VMEM)
HBM = pl.BlockSpec(memory_space=pltpu.HBM)
GROUP = 512
GROUPS = 4


def group_of(ref, group):
    return ref.at[:, pl.ds(GROUP * group, GROUP)]


def start_loading(cov_ref, held_ref, sems, first):
    copies = [
        pltpu.make_async_copy(group_of(cov_ref, g), held_ref.at[g], sems.at[g])
        for g in range(first, GROUPS)
    ]
    for copy in copies:
        copy.start()
    return copies


def params(mib):
    return pltpu.CompilerParams(vmem_limit_bytes=int(mib * 1048576))


def load(cov, count):
    def load_kernel(cov_ref, out_ref, sems):
        copies = [
            pltpu.make_async_copy(group_of(cov_ref, g), out_ref.at[g], sems.at[g])
            for g in range(count)
        ]
        for copy in copies:
            copy.start()
        for copy in copies:
            copy.wait()

    return pl.pallas_call(
        load_kernel,
        in_specs=[HBM],
        out_specs=VMEM,
        out_shape=jax.ShapeDtypeStruct((count, 512, GROUP), f32),
        scratch_shapes=[pltpu.SemaphoreType.DMA((count,))],
        compiler_params=params(16),
        name="fetch",
    )(cov)


EARLY = 3
AGAIN = 2


def product_kernel(jac_ref, early_ref, cov_ref, out_refs, own_ref, late_ref, whole_ref, sems):
    copies = [
        pltpu.make_async_copy(group_of(cov_ref, g), late_ref.at[g - EARLY], sems.at[g - EARLY])
        for g in range(EARLY, GROUPS)
    ]
    for copy in copies:
        copy.start()
    col = lax.axis_index("col")
    core = lax.rem(col, 2)
    blocks = [paired(jac_ref[2 * q], jac_ref[2 * q + 1]) for q in range(4)]
    own = blocks[0]
    for q in range(1, 4):
        own = jnp.where(col // 2 == q, blocks[q], own)
    own_ref[...] = own
    jac = jnp.concatenate(blocks, axis=1)
    dims = ((1,), (0,))
    for group in range(GROUPS):
        if group >= EARLY:
            copies[group - EARLY].wait()
        hi, low = halves(early_ref[group] if group < EARLY else late_ref[group - EARLY])
        part = dot(jac, low, dims) + dot(jac, hi, dims)
        for step in range(GROUP // 128):
            for h in range(2):
                x, z = piece_at(GROUP // 128 * group + step, h, core)
                whole_ref[x, z] = part[32 * h : 32 * h + 32, 128 * step : 128 * step + 128]
    x = lax.axis_index("row") // 8
    for turn in range(4):
        out_refs[turn][...] = whole_ref[lax.rem(x + turn, 4)]


def product(jac, early, cov):
    return pl.pallas_call(
        product_kernel,
        in_specs=[VMEM, VMEM, HBM],
        out_specs=[[VMEM] * 4, VMEM],
        out_shape=[
            [jax.ShapeDtypeStruct((8, 32, 128), f32)] * 4,
            jax.ShapeDtypeStruct((64, 128), bf16),
        ],
        scratch_shapes=[
            pltpu.VMEM((GROUPS - EARLY, 512, GROUP), f32),
            pltpu.VMEM((4, 8, 32, 128), f32),
            pltpu.SemaphoreType.DMA((GROUPS - EARLY,)),
        ],
        compiler_params=params(16),
        name="product",
    )(jac, early, cov)


def add_kernel(first_ref, second_ref, third_ref, fourth_ref, out_ref):
    out_ref[...] = (first_ref[...] + second_ref[...]) + (third_ref[...] + fourth_ref[...])


def add(parts):
    return pl.pallas_call(
        add_kernel,
        in_specs=[VMEM] * 4,
        out_specs=VMEM,
        out_shape=jax.ShapeDtypeStruct((8, 32, 128), f32),
        compiler_params=params(8),
        name="add",
    )(*parts)


def reduce_kernel(parts_ref, jac_ref, own_ref, line_ref):
    total = jnp.sum(parts_ref[...], axis=0)
    own_ref[...] = total
    dims = ((1,), (1,))
    hi, mid, low = thirds(total)
    jac = jac_ref[...]
    gram = dot(jac, low, dims) + dot(jac, mid, dims) + dot(jac, hi, dims)
    packed = jnp.concatenate([gram[16 * q : 16 * q + 16] for q in range(4)], axis=1)
    line_ref[:, :32] = jnp.broadcast_to(total[None], (8, 32, 128))
    line_ref[:, 32:] = jnp.broadcast_to(packed[None], (8, 16, 128))


def reduce(parts, jac):
    return pl.pallas_call(
        reduce_kernel,
        in_specs=[VMEM] * 2,
        out_specs=[VMEM] * 2,
        out_shape=[
            jax.ShapeDtypeStruct((32, 128), f32),
            jax.ShapeDtypeStruct((8, 48, 128), f32),
        ],
        compiler_params=params(8),
        name="reduce",
    )(parts, jac)


def spread_kernel(parts_ref, natural_ref, line_ref, out_ref):
    line_ref[...] = parts_ref[:, :32]
    out_ref[:, :32] = jnp.broadcast_to(natural_ref[...][None], (8, 32, 128))
    for h in range(2):
        total = parts_ref[h, 32:]
        for z in range(h + 2, 8, 2):
            total = total + parts_ref[z, 32:]
        out_ref[:, 32 + 16 * h : 48 + 16 * h] = jnp.broadcast_to(total[None], (8, 16, 128))


def spread(parts, natural):
    return pl.pallas_call(
        spread_kernel,
        in_specs=[VMEM] * 2,
        out_specs=[VMEM] * 2,
        out_shape=[
            jax.ShapeDtypeStruct((8, 32, 128), f32),
            jax.ShapeDtypeStruct((8, 64, 128), f32),
        ],
        compiler_params=params(4),
        name="spread",
    )(parts, natural)


def gather_kernel(rows_ref, out_ref):
    total = rows_ref[0, 32:]
    for c in range(1, 8):
        total = total + rows_ref[c, 32:]
    out_ref[...] = total


def gather(rows):
    return pl.pallas_call(
        gather_kernel,
        in_specs=[VMEM],
        out_specs=VMEM,
        out_shape=jax.ShapeDtypeStruct((32, 128), f32),
        compiler_params=params(4),
        name="gather",
    )(rows)


PANEL = 8


def inverse_factor(first, second):
    left = jnp.concatenate([first[:, 32 * q : 32 * q + 32] for q in range(4)], axis=0)
    right = jnp.concatenate([second[:, 32 * q : 32 * q + 32] for q in range(4)], axis=0)
    gram = jnp.concatenate([left, right, jnp.zeros((64, 64), f32)], axis=1)
    rows = lax.broadcasted_iota(jnp.int32, (64, 128), 0)
    lanes = lax.broadcasted_iota(jnp.int32, (64, 128), 1)
    shift = jnp.where(rows < 32, lam_start, lam_start * lam_next).astype(f32)
    work = gram + jnp.where(rows == lanes, shift, 0.0) + jnp.where(rows + 64 == lanes, 1.0, 0.0)
    done = []
    for start in range(0, 64, PANEL):
        pivots = [work[j : j + 1, :] for j in range(PANEL)]
        rest = work[PANEL:, :]
        low = rest.shape[0]
        spots = range(start, start + PANEL)
        entry = {
            (i, j): jnp.broadcast_to(pivots[i][:, start + j : start + j + 1], (1, 128))
            for i in range(PANEL)
            for j in range(i + 1)
        }
        columns = [jnp.broadcast_to(rest[:, j : j + 1], (low, 128)) for j in spots] if low else []
        for j in range(PANEL):
            inverse = 1.0 / entry[j, j]
            factors = {i: entry[i, j] * inverse for i in range(j + 1, PANEL)}
            for i in range(j + 1, PANEL):
                pivots[i] = pivots[i] - factors[i] * pivots[j]
                for m in range(j + 1, i + 1):
                    entry[i, m] = entry[i, m] - factors[m] * entry[i, j]
                if low:
                    columns[i] = columns[i] - factors[i] * columns[j]
            done.append(pivots[j] * lax.rsqrt(entry[j, j]))
            if low:
                rest = rest - columns[j] * (pivots[j] * inverse)
        work = rest
    return jnp.concatenate(done, axis=0)[:, 64:]


def update_kernel(
    early_ref,
    cov_ref,
    line_refs,
    gram_refs,
    rows_ref,
    first_ref,
    second_ref,
    out_ref,
    inc_ref,
    held_ref,
    cols_ref,
    in_sems,
    out_sems,
):
    loads = start_loading(cov_ref, held_ref, in_sems, AGAIN)
    col = lax.axis_index("col")
    core = lax.rem(col, 2)
    x = lax.axis_index("row") // 8
    for turn, line_ref in enumerate(line_refs):
        cols_ref[lax.rem(x + turn, 4)] = line_ref[...]
    total = (gram_refs[0][...] + gram_refs[1][...]) + (gram_refs[2][...] + gram_refs[3][...])
    first, second = total[:16], total[16:]
    inverse = inverse_factor(first, second)
    hi, mid, low = thirds(inverse)
    inverse_parts = jnp.concatenate([hi, hi, hi, mid, mid, low], axis=1)

    def whitened(block):
        hi, mid, low = thirds(block)
        parts = jnp.concatenate([hi, mid, low, hi, mid, hi], axis=0)
        return dot(inverse_parts, parts, ((1,), (0,)))

    rows = whitened(
        jnp.concatenate(
            [
                jnp.concatenate([rows_ref[2 * t, :32], rows_ref[2 * t + 1, :32]], axis=0)
                for t in range(4)
            ],
            axis=1,
        )
    )
    hi, low = halves(rows.T)
    left = jnp.concatenate([hi, hi, low, low], axis=1)
    errors = jnp.concatenate([first_ref[...], second_ref[...]], axis=1)
    weights = jnp.sum(inverse * errors, axis=1, keepdims=True)
    inc = jnp.sum(rows * weights, axis=0, keepdims=True)
    own = jnp.zeros((1, 128), f32)
    for tile in range(4):
        own = own + jnp.where(col // 2 == tile, inc[:, 128 * tile : 128 * tile + 128], 0.0)
    inc_ref[...] = jnp.where(core == 1, own[:, 64:], own[:, :64])

    cols = whitened(
        jnp.concatenate(
            [
                jnp.concatenate([cols_ref[piece_at(tile, h, core)] for h in range(2)], axis=0)
                for tile in range(16)
            ],
            axis=1,
        )
    )
    hi, low = halves(cols)
    right = jnp.concatenate([hi, low, hi, low], axis=0)
    stores = []
    for group in range(GROUPS):
        change = dot(left, right[:, GROUP * group : GROUP * group + GROUP], ((1,), (0,)))
        if group >= AGAIN:
            loads[group - AGAIN].wait()
        old = early_ref[group] if group < AGAIN else held_ref[group]
        held_ref[group] = (old - change) * (1.0 / (lam_start * lam_next))
        store = pltpu.make_async_copy(
            held_ref.at[group], group_of(out_ref, group), out_sems.at[group]
        )
        store.start()
        stores.append(store)
    for store in stores:
        store.wait()


def update(early, cov, lines, grams, rows, first, second):
    return pl.pallas_call(
        update_kernel,
        in_specs=[VMEM, HBM, [VMEM] * 4, [VMEM] * 4] + [VMEM] * 3,
        out_specs=[HBM, VMEM],
        out_shape=[
            jax.ShapeDtypeStruct((512, 2048), f32),
            jax.ShapeDtypeStruct((1, 64), f32),
        ],
        scratch_shapes=[
            pltpu.VMEM((GROUPS, 512, GROUP), f32),
            pltpu.VMEM((4, 8, 32, 128), f32),
            pltpu.SemaphoreType.DMA((GROUPS,)),
            pltpu.SemaphoreType.DMA((GROUPS,)),
        ],
        compiler_params=params(16),
        name="update",
    )(early, cov, lines, grams, rows, first, second)


def exchange(array, axis, groups=None):
    return lax.all_to_all(array, axis, 0, 0, axis_index_groups=groups, tiled=True)


Z_LINES = [[8 * x + z for z in range(8)] for x in range(4)]


def copies_of(first, second):
    pair = [jnp.broadcast_to(array[None], (8, 32, 64)) for array in (first, second)]
    return jnp.concatenate(pair, axis=2)


def moved(array, turn):
    return lax.ppermute(array, "row", [(r, (r + 8 * turn) % 32) for r in range(32)])


def along_x(array):
    return [array] + [moved(array, 4 - turn) for turn in (1, 2, 3)]


def body(covariance, first_jacobian, second_jacobian, first_residuals, second_residuals):
    both = ("row", "col")
    jac_rows = exchange(copies_of(first_jacobian, second_jacobian), "col")
    covariance = pltpu.with_memory_space_constraint(covariance, pltpu.HBM)
    held = load(covariance, EARLY)
    parts, jac_own = product(jac_rows, held, covariance)
    parts = parts[:1] + [moved(parts[turn], turn) for turn in (1, 2, 3)]
    parts = add(parts)
    parts = exchange(parts, "row", Z_LINES)
    jac_piece = lax.ppermute(jac_own, both, reversed_pairs(to_row_block()))
    own, line = reduce(parts, jac_piece)
    line = exchange(line, "row", Z_LINES)
    natural = lax.ppermute(own, both, to_row_block())
    line, rows = spread(line, natural)
    rows = exchange(rows, "col")
    lines = along_x(line)
    held = load(covariance, AGAIN)
    grams = along_x(gather(rows))
    out, increment = update(
        held, covariance, lines, grams, rows, first_residuals[None], second_residuals[None]
    )
    return out, increment[0]


def solution(mesh):
    return jax.shard_map(
        body,
        mesh=mesh,
        in_specs=(P("row", "col"), P(None, ("row", "col")), P(None, ("row", "col")), P(), P()),
        out_specs=(P("row", "col"), P(("row", "col"))),
        check_vma=False,
    )
```

```python
import jax
import jax.numpy as jnp
from jax import lax
from jax.experimental import pallas as pl
from jax.experimental.pallas import tpu as pltpu
from jax.sharding import PartitionSpec as P


lam_start = 0.98
forget_rate = 0.9987
lam_next = forget_rate * lam_start + (1.0 - forget_rate)

f32 = jnp.float32
bf16 = jnp.bfloat16


def device(x, y, z, k):
    return (x * 8 + z) * 8 + y * 2 + k


def to_row_block():
    pairs = []
    for x in range(4):
        for y in range(4):
            for z in range(8):
                for k in range(2):
                    i = ((z + 2 + 4 * k) % 8) // 2
                    target = device(y, (x + 2) % 4, 4 * k + i, z % 2)
                    pairs.append((device(x, y, z, k), target))
    return pairs


def reversed_pairs(pairs):
    return [(b, a) for a, b in pairs]


def piece_at(tile, h, core):
    return (tile % 4 + 2) % 4, lax.rem(2 * (tile // 4) + h + 6 + 4 * core, 8)


def halves(value):
    hi = value.astype(bf16)
    return hi, (value - hi.astype(f32)).astype(bf16)


def thirds(value):
    hi = value.astype(bf16)
    rest = value - hi.astype(f32)
    mid = rest.astype(bf16)
    return hi, mid, (rest - mid.astype(f32)).astype(bf16)


def dot(a, b, dims):
    return lax.dot_general(a, b, (dims, ((), ())), preferred_element_type=f32)


def paired(even, odd):
    even, odd = even.astype(f32), odd.astype(f32)
    low = lax.broadcasted_iota(jnp.int32, even.shape, 1) < 64
    top = jnp.where(low, even, pltpu.roll(odd, 64, 1))
    bottom = jnp.where(low, pltpu.roll(even, 64, 1), odd)
    return jnp.concatenate([top, bottom], axis=0).astype(bf16)


VMEM = pl.BlockSpec(memory_space=pltpu.VMEM)
HBM = pl.BlockSpec(memory_space=pltpu.HBM)
GROUP = 512
GROUPS = 4


def group_of(ref, group):
    return ref.at[:, pl.ds(GROUP * group, GROUP)]


def start_loading(cov_ref, held_ref, sems, first):
    copies = [
        pltpu.make_async_copy(group_of(cov_ref, g), held_ref.at[g], sems.at[g])
        for g in range(first, GROUPS)
    ]
    for copy in copies:
        copy.start()
    return copies


def params(mib):
    return pltpu.CompilerParams(vmem_limit_bytes=int(mib * 1048576))


def load(cov, count):
    def load_kernel(cov_ref, out_ref, sems):
        copies = [
            pltpu.make_async_copy(group_of(cov_ref, g), out_ref.at[g], sems.at[g])
            for g in range(count)
        ]
        for copy in copies:
            copy.start()
        for copy in copies:
            copy.wait()

    return pl.pallas_call(
        load_kernel,
        in_specs=[HBM],
        out_specs=VMEM,
        out_shape=jax.ShapeDtypeStruct((count, 512, GROUP), f32),
        scratch_shapes=[pltpu.SemaphoreType.DMA((count,))],
        compiler_params=params(16),
        name="fetch",
    )(cov)


EARLY = 3
AGAIN = 2


def product_kernel(jac_ref, early_ref, cov_ref, out_refs, own_ref, late_ref, whole_ref, sems):
    copies = [
        pltpu.make_async_copy(group_of(cov_ref, g), late_ref.at[g - EARLY], sems.at[g - EARLY])
        for g in range(EARLY, GROUPS)
    ]
    for copy in copies:
        copy.start()
    col = lax.axis_index("col")
    core = lax.rem(col, 2)
    blocks = [paired(jac_ref[2 * q], jac_ref[2 * q + 1]) for q in range(4)]
    own = blocks[0]
    for q in range(1, 4):
        own = jnp.where(col // 2 == q, blocks[q], own)
    own_ref[...] = own
    jac = jnp.concatenate(blocks, axis=1)
    dims = ((1,), (0,))
    for group in range(GROUPS):
        if group >= EARLY:
            copies[group - EARLY].wait()
        hi, low = halves(early_ref[group] if group < EARLY else late_ref[group - EARLY])
        part = dot(jac, low, dims) + dot(jac, hi, dims)
        for step in range(GROUP // 128):
            for h in range(2):
                x, z = piece_at(GROUP // 128 * group + step, h, core)
                whole_ref[x, z] = part[32 * h : 32 * h + 32, 128 * step : 128 * step + 128]
    x = lax.axis_index("row") // 8
    for turn in range(4):
        out_refs[turn][...] = whole_ref[lax.rem(x + turn, 4)]


def product(jac, early, cov):
    return pl.pallas_call(
        product_kernel,
        in_specs=[VMEM, VMEM, HBM],
        out_specs=[[VMEM] * 4, VMEM],
        out_shape=[
            [jax.ShapeDtypeStruct((8, 32, 128), f32)] * 4,
            jax.ShapeDtypeStruct((64, 128), bf16),
        ],
        scratch_shapes=[
            pltpu.VMEM((GROUPS - EARLY, 512, GROUP), f32),
            pltpu.VMEM((4, 8, 32, 128), f32),
            pltpu.SemaphoreType.DMA((GROUPS - EARLY,)),
        ],
        compiler_params=params(16),
        name="product",
    )(jac, early, cov)


def add_kernel(first_ref, second_ref, third_ref, fourth_ref, out_ref):
    out_ref[...] = (first_ref[...] + second_ref[...]) + (third_ref[...] + fourth_ref[...])


def add(parts):
    return pl.pallas_call(
        add_kernel,
        in_specs=[VMEM] * 4,
        out_specs=VMEM,
        out_shape=jax.ShapeDtypeStruct((8, 32, 128), f32),
        compiler_params=params(8),
        name="add",
    )(*parts)


def reduce_kernel(parts_ref, jac_ref, own_ref, line_ref):
    total = jnp.sum(parts_ref[...], axis=0)
    own_ref[...] = total
    dims = ((1,), (1,))
    hi, mid, low = thirds(total)
    jac = jac_ref[...]
    gram = dot(jac, low, dims) + dot(jac, mid, dims) + dot(jac, hi, dims)
    packed = jnp.concatenate([gram[16 * q : 16 * q + 16] for q in range(4)], axis=1)
    line_ref[:, :32] = jnp.broadcast_to(total[None], (8, 32, 128))
    line_ref[:, 32:] = jnp.broadcast_to(packed[None], (8, 16, 128))


def reduce(parts, jac):
    return pl.pallas_call(
        reduce_kernel,
        in_specs=[VMEM] * 2,
        out_specs=[VMEM] * 2,
        out_shape=[
            jax.ShapeDtypeStruct((32, 128), f32),
            jax.ShapeDtypeStruct((8, 48, 128), f32),
        ],
        compiler_params=params(8),
        name="reduce",
    )(parts, jac)


def line_kernel(parts_ref, out_ref):
    out_ref[...] = parts_ref[:, :32]


def line_of(parts):
    return pl.pallas_call(
        line_kernel,
        in_specs=[VMEM],
        out_specs=VMEM,
        out_shape=jax.ShapeDtypeStruct((8, 32, 128), f32),
        compiler_params=params(4),
        name="line",
    )(parts)


def spread_kernel(parts_ref, natural_ref, out_ref):
    out_ref[:, :32] = jnp.broadcast_to(natural_ref[...][None], (8, 32, 128))
    for h in range(2):
        total = parts_ref[h, 32:]
        for z in range(h + 2, 8, 2):
            total = total + parts_ref[z, 32:]
        out_ref[:, 32 + 16 * h : 48 + 16 * h] = jnp.broadcast_to(total[None], (8, 16, 128))


def spread(parts, natural):
    return pl.pallas_call(
        spread_kernel,
        in_specs=[VMEM] * 2,
        out_specs=VMEM,
        out_shape=jax.ShapeDtypeStruct((8, 64, 128), f32),
        compiler_params=params(4),
        name="spread",
    )(parts, natural)


def gather_kernel(rows_ref, out_ref):
    total = rows_ref[0, 32:]
    for c in range(1, 8):
        total = total + rows_ref[c, 32:]
    out_ref[...] = total


def gather(rows):
    return pl.pallas_call(
        gather_kernel,
        in_specs=[VMEM],
        out_specs=VMEM,
        out_shape=jax.ShapeDtypeStruct((32, 128), f32),
        compiler_params=params(4),
        name="gather",
    )(rows)


PANEL = 8


def inverse_factor(first, second):
    left = jnp.concatenate([first[:, 32 * q : 32 * q + 32] for q in range(4)], axis=0)
    right = jnp.concatenate([second[:, 32 * q : 32 * q + 32] for q in range(4)], axis=0)
    gram = jnp.concatenate([left, right, jnp.zeros((64, 64), f32)], axis=1)
    rows = lax.broadcasted_iota(jnp.int32, (64, 128), 0)
    lanes = lax.broadcasted_iota(jnp.int32, (64, 128), 1)
    shift = jnp.where(rows < 32, lam_start, lam_start * lam_next).astype(f32)
    work = gram + jnp.where(rows == lanes, shift, 0.0) + jnp.where(rows + 64 == lanes, 1.0, 0.0)
    done = []
    for start in range(0, 64, PANEL):
        pivots = [work[j : j + 1, :] for j in range(PANEL)]
        rest = work[PANEL:, :]
        low = rest.shape[0]
        spots = range(start, start + PANEL)
        entry = {
            (i, j): jnp.broadcast_to(pivots[i][:, start + j : start + j + 1], (1, 128))
            for i in range(PANEL)
            for j in range(i + 1)
        }
        columns = [jnp.broadcast_to(rest[:, j : j + 1], (low, 128)) for j in spots] if low else []
        for j in range(PANEL):
            inverse = 1.0 / entry[j, j]
            factors = {i: entry[i, j] * inverse for i in range(j + 1, PANEL)}
            for i in range(j + 1, PANEL):
                pivots[i] = pivots[i] - factors[i] * pivots[j]
                for m in range(j + 1, i + 1):
                    entry[i, m] = entry[i, m] - factors[m] * entry[i, j]
                if low:
                    columns[i] = columns[i] - factors[i] * columns[j]
            done.append(pivots[j] * lax.rsqrt(entry[j, j]))
            if low:
                rest = rest - columns[j] * (pivots[j] * inverse)
        work = rest
    return jnp.concatenate(done, axis=0)[:, 64:]


def update_kernel(
    early_ref,
    cov_ref,
    line_refs,
    gram_refs,
    rows_ref,
    first_ref,
    second_ref,
    out_ref,
    inc_ref,
    held_ref,
    cols_ref,
    in_sems,
    out_sems,
):
    loads = start_loading(cov_ref, held_ref, in_sems, AGAIN)
    col = lax.axis_index("col")
    core = lax.rem(col, 2)
    x = lax.axis_index("row") // 8
    for turn, line_ref in enumerate(line_refs):
        cols_ref[lax.rem(x + turn, 4)] = line_ref[...]
    total = (gram_refs[0][...] + gram_refs[1][...]) + (gram_refs[2][...] + gram_refs[3][...])
    first, second = total[:16], total[16:]
    inverse = inverse_factor(first, second)
    hi, mid, low = thirds(inverse)
    inverse_parts = jnp.concatenate([hi, hi, hi, mid, mid, low], axis=1)

    def whitened(block):
        hi, mid, low = thirds(block)
        parts = jnp.concatenate([hi, mid, low, hi, mid, hi], axis=0)
        return dot(inverse_parts, parts, ((1,), (0,)))

    rows = whitened(
        jnp.concatenate(
            [
                jnp.concatenate([rows_ref[2 * t, :32], rows_ref[2 * t + 1, :32]], axis=0)
                for t in range(4)
            ],
            axis=1,
        )
    )
    hi, low = halves(rows.T)
    left = jnp.concatenate([hi, hi, low, low], axis=1)
    errors = jnp.concatenate([first_ref[...], second_ref[...]], axis=1)
    weights = jnp.sum(inverse * errors, axis=1, keepdims=True)
    inc = jnp.sum(rows * weights, axis=0, keepdims=True)
    own = jnp.zeros((1, 128), f32)
    for tile in range(4):
        own = own + jnp.where(col // 2 == tile, inc[:, 128 * tile : 128 * tile + 128], 0.0)
    inc_ref[...] = jnp.where(core == 1, own[:, 64:], own[:, :64])

    cols = whitened(
        jnp.concatenate(
            [
                jnp.concatenate([cols_ref[piece_at(tile, h, core)] for h in range(2)], axis=0)
                for tile in range(16)
            ],
            axis=1,
        )
    )
    hi, low = halves(cols)
    right = jnp.concatenate([hi, low, hi, low], axis=0)
    stores = []
    for group in range(GROUPS):
        change = dot(left, right[:, GROUP * group : GROUP * group + GROUP], ((1,), (0,)))
        if group >= AGAIN:
            loads[group - AGAIN].wait()
        old = early_ref[group] if group < AGAIN else held_ref[group]
        held_ref[group] = (old - change) * (1.0 / (lam_start * lam_next))
        store = pltpu.make_async_copy(
            held_ref.at[group], group_of(out_ref, group), out_sems.at[group]
        )
        store.start()
        stores.append(store)
    for store in stores:
        store.wait()


def update(early, cov, lines, grams, rows, first, second):
    return pl.pallas_call(
        update_kernel,
        in_specs=[VMEM, HBM, [VMEM] * 4, [VMEM] * 4] + [VMEM] * 3,
        out_specs=[HBM, VMEM],
        out_shape=[
            jax.ShapeDtypeStruct((512, 2048), f32),
            jax.ShapeDtypeStruct((1, 64), f32),
        ],
        scratch_shapes=[
            pltpu.VMEM((GROUPS, 512, GROUP), f32),
            pltpu.VMEM((4, 8, 32, 128), f32),
            pltpu.SemaphoreType.DMA((GROUPS,)),
            pltpu.SemaphoreType.DMA((GROUPS,)),
        ],
        compiler_params=params(16),
        name="update",
    )(early, cov, lines, grams, rows, first, second)


def exchange(array, axis, groups=None):
    return lax.all_to_all(array, axis, 0, 0, axis_index_groups=groups, tiled=True)


Z_LINES = [[8 * x + z for z in range(8)] for x in range(4)]


def moved(array, turn):
    return lax.ppermute(array, "row", [(r, (r + 8 * turn) % 32) for r in range(32)])


def along_x(array):
    return [array] + [moved(array, 4 - turn) for turn in (1, 2, 3)]


def body(covariance, first_jacobian, second_jacobian, first_residuals, second_residuals):
    both = ("row", "col")
    jac = jnp.concatenate([first_jacobian, second_jacobian], axis=1)
    jac_rows = exchange(jnp.broadcast_to(jac[None], (8, 32, 128)), "col")
    covariance = pltpu.with_memory_space_constraint(covariance, pltpu.HBM)
    held = load(covariance, EARLY)
    parts, jac_own = product(jac_rows, held, covariance)
    parts = parts[:1] + [moved(parts[turn], turn) for turn in (1, 2, 3)]
    parts = add(parts)
    parts = exchange(parts, "row", Z_LINES)
    jac_piece = lax.ppermute(jac_own, both, reversed_pairs(to_row_block()))
    own, line = reduce(parts, jac_piece)
    line = exchange(line, "row", Z_LINES)
    natural = lax.ppermute(own, both, to_row_block())
    rows = spread(line, natural)
    line = line_of(line)
    rows = exchange(rows, "col")
    lines = along_x(line)
    held = load(covariance, AGAIN)
    grams = along_x(gather(rows))
    out, increment = update(
        held, covariance, lines, grams, rows, first_residuals[None], second_residuals[None]
    )
    return out, increment[0]


def solution(mesh):
    return jax.shard_map(
        body,
        mesh=mesh,
        in_specs=(P("row", "col"), P(None, ("row", "col")), P(None, ("row", "col")), P(), P()),
        out_specs=(P("row", "col"), P(("row", "col"))),
        check_vma=False,
    )
```
